512 devices in a mesh: mem: 8 (over x, core), gx: 4 (over z_hi), gy: 16 (over z_lo, y).
Axes of the slice: x: 4, y: 4, z: 16 (z_hi: 4, z_lo: 4; z = z_hi * 4 + z_lo), core: 2. Of those that a mesh axis runs over, the one named last changes fastest.
Arguments:
- control: float32 [64, 3, 512, 512], P('mem', None, 'gy', 'gx'), may hold values from -6 to 6
- perturb: bfloat16 [64, 6, 3, 512, 512], P('mem', None, None, 'gy', 'gx'), may hold values from -6 to 6
- obs_count: int32 [3, 512, 512], P(None, 'gy', 'gx'), may hold values from 0 to 3
- obs_weight: float32 [6], replicated, may hold values from 0.3 to 3
- diffusivity: float32 [3, 512, 512], P(None, 'gy', 'gx'), may hold values from 0.12 to 0.24
Outputs:
- hess_product: float32 [64, 3, 512, 512], P('mem', None, 'gy', 'gx')
The draws below stay inside these ranges and needn't reach their ends.
All inputs are finite; a program needn't handle non-finite values.
Results may differ from the reference program's by a relative error of at most 0.0003.
Values sent between devices are 32-bit elements; how exact they have to be, the bound alone decides.
No kernel may reach another device: no remote copies, remote signals or barrier semaphores. Data moves between devices by JAX's collectives and lax.ppermute only.
A program may use at most 64 MiB of HBM per device.

```python
import math
import jax
import jax.numpy as jnp
from jax import lax

VAR = 6
LEV = 3
STEPS = 4
MEMBERS = 64
NX = 512
NY = 512


def set_ends(drawn, rng, low, high):
    index_at = [jax.random.randint(jax.random.fold_in(rng, axis), (), 0, length) for axis, length in enumerate(drawn.shape)]
    widest = drawn.shape.index(max(drawn.shape))
    beside = index_at[:widest] + [(index_at[widest] + 1) % drawn.shape[widest]] + index_at[widest + 1:]
    return drawn.at[tuple(index_at)].set(low).at[tuple(beside)].set(high)


def steps_of(stream_key, extent, cuts, smallest, top_value):
    def one(axis_at, blocks):
        steps = jax.random.uniform(jax.random.fold_in(jax.random.fold_in(stream_key, 6), axis_at), (blocks,), jnp.float32, smallest / len(cuts), top_value / len(cuts))
        return jnp.repeat(jnp.exp(steps), extent[axis_at] // blocks).reshape((-1,) + (1,) * (len(extent) - axis_at - 1))

    factor_of = one(*cuts[0])
    for cut in cuts[1:]:
        factor_of = factor_of * one(*cut)
    return factor_of


def bell_draw(key, extent, width, bound, split=(), held_as=jnp.bfloat16):
    array = width * jax.random.normal(key, extent, jnp.float32)
    if split:
        array = array * steps_of(key, extent, split, -0.22, 0.18)
    return jnp.clip(array, -bound, bound).astype(held_as)


def setup_inputs(seed: int = 0) -> dict:
    keys = jax.random.split(jax.random.key(seed), 6)
    control = bell_draw(keys[0], (MEMBERS, LEV, NY, NX), 1.0, 6.0, ((0, 8), (2, 16), (3, 4)), jnp.float32)
    perturb = bell_draw(keys[1], (MEMBERS, VAR, LEV, NY, NX), 1.0, 6.0, ((0, 8), (3, 16), (4, 4)))
    obs_count = set_ends(jax.random.randint(keys[2], (LEV, NY, NX), 0, 4), jax.random.fold_in(keys[2], 1), 0, 3).astype(jnp.int32)
    obs_weight = jnp.clip(jnp.exp(jax.random.uniform(keys[3], (VAR,), jnp.float32, math.log(0.3), math.log(3.0))), 0.3, 3.0)
    diffusivity = jnp.clip(0.12 + 0.12 * jax.random.uniform(keys[4], (LEV, NY, NX), jnp.float32) ** steps_of(keys[4], (LEV, NY, NX), ((1, 16), (2, 4)), -0.2, 0.2), 0.12, 0.24)
    return {"control": control, "perturb": perturb, "obs_count": obs_count, "obs_weight": obs_weight, "diffusivity": diffusivity}


def laplace(padded):
    return padded[..., 2:, 1:-1] + padded[..., :-2, 1:-1] + padded[..., 1:-1, 2:] + padded[..., 1:-1, :-2] - 4.0 * padded[..., 1:-1, 1:-1]

def zero_rim(field):
    widths = [(0, 0)] * (field.ndim - 2) + [(1, 1), (1, 1)]
    return jnp.pad(field, widths)

def reference(control, perturb, obs_count, obs_weight, diffusivity):
    ensemble_scale = 1.0 / math.sqrt(MEMBERS - 1)
    spread = control
    for step_index in range(STEPS):
        spread = spread + diffusivity * laplace(zero_rim(spread))

    def add_member(total, pieces):
        member_pert, member_field = pieces
        return (total + member_pert.astype(jnp.float32) * member_field[None], None)
    start_sum = jnp.zeros((VAR, LEV, NY, NX), jnp.float32)
    increment, unused = lax.scan(add_member, start_sum, (perturb, spread))
    increment = increment * ensemble_scale
    weighted = obs_count.astype(jnp.float32)[None] * obs_weight[:, None, None, None] * increment

    def project(member_pert):
        return lax.optimization_barrier(jnp.sum(member_pert.astype(jnp.float32) * weighted, axis=0)) * ensemble_scale
    back = lax.map(project, perturb)
    for step_index in range(STEPS):
        back = back + laplace(zero_rim(diffusivity * back))
    return control + back
```

```python
import math

import jax
import jax.numpy as jnp
from jax import lax
from jax.experimental import pallas as pl
from jax.experimental.pallas import tpu as pltpu
from jax.sharding import PartitionSpec as P

STEPS = 4
LANES = 128


def exchange(last, first, axis):
    size = lax.axis_size(axis)
    up = [(i, i + 1) for i in range(size - 1)]
    down = [(j, i) for i, j in up]
    return lax.ppermute(last, axis, up), lax.ppermute(first, axis, down)


def lane_ids(rows):
    return lax.broadcasted_iota(jnp.int32, (rows, LANES), 1)


def pack_columns(planes, rows):
    group = lane_ids(rows) // STEPS
    first = jnp.zeros((rows, LANES), jnp.float32)
    last = jnp.zeros((rows, LANES), jnp.float32)
    for p, plane in enumerate(planes):
        first = jnp.where(group == p, pltpu.roll(plane, (STEPS * p) % LANES, 1), first)
        last = jnp.where(group == p, pltpu.roll(plane, (STEPS * p + STEPS) % LANES, 1), last)
    return first, last


def pack_kernel(control, diffusivity, first, last):
    count, rows, _ = control.shape
    planes = [control[p] for p in range(count)] + [diffusivity[l] for l in range(diffusivity.shape[0])]
    first[...], last[...] = pack_columns(planes, rows)


def side_lanes(west, east, p, rows):
    lane = lane_ids(rows)
    east_part = pltpu.roll(east, lax.rem(2 * LANES - STEPS * p, LANES), 1)
    west_part = pltpu.roll(west, lax.rem(2 * LANES - STEPS - STEPS * p, LANES), 1)
    return jnp.where(lane < STEPS, east_part, jnp.where(lane >= LANES - STEPS, west_part, 0.0))


def widened(main, sides, rim, rim_sides):
    top = jnp.concatenate([main, rim], axis=0)
    side = jnp.concatenate([sides, rim_sides], axis=0)
    return jnp.concatenate([top, side], axis=1)


def neighbours(field):
    rows, lanes = field.shape
    return (
        pltpu.roll(field, 1, 0)
        + pltpu.roll(field, rows - 1, 0)
        + pltpu.roll(field, 1, 1)
        + pltpu.roll(field, lanes - 1, 1)
    )


def spread_kernel(levels, control, diffusivity, west, east, rim, perturb, partial, wide_diff, spread):
    count, rows, _ = control.shape
    members = count // levels
    variables = perturb.shape[1]

    def wide(main, p):
        sides = side_lanes(west[...], east[...], p, rows)
        rim_sides = side_lanes(rim[count + levels], rim[count + levels + 1], p, 2 * STEPS)
        return widened(main, sides, rim[p], rim_sides)

    for l in range(levels):
        wide_diff[l] = wide(diffusivity[l], count + l)

    def one(m, carry):
        for l in range(levels):
            field = wide(control[m * levels + l], m * levels + l)
            for _ in range(STEPS):
                field = field + wide_diff[l] * (neighbours(field) - 4.0 * field)
            spread[m * levels + l] = field[:rows, :LANES]
        return carry

    lax.fori_loop(0, members, one, 0)
    for v in range(variables):
        for l in range(levels):
            total = perturb[0, v, l].astype(jnp.float32) * spread[l]
            for m in range(1, members):
                total = total + perturb[m, v, l].astype(jnp.float32) * spread[m * levels + l]
            partial[v * levels + l] = total


def back_kernel(scale, increment, obs_count, obs_weight, perturb, back, first, last, weighted):
    members, variables, levels, rows, _ = perturb.shape
    for l in range(levels):
        seen = obs_count[l].astype(jnp.float32) * (scale * scale)
        for v in range(variables):
            weighted[v * levels + l] = seen * obs_weight[v] * increment[v * levels + l]
    planes = []
    for m in range(members):
        for l in range(levels):
            total = perturb[m, 0, l].astype(jnp.float32) * weighted[l]
            for v in range(1, variables):
                total = total + perturb[m, v, l].astype(jnp.float32) * weighted[v * levels + l]
            back[m * levels + l] = total
    planes = [back[p] for p in range(members * levels)]
    first[...], last[...] = pack_columns(planes, rows)


def adjoint_kernel(levels, control, back, wide_diff, west, east, rim, out):
    count, rows, _ = back.shape

    def one(m, carry):
        for l in range(levels):
            p = m * levels + l
            sides = side_lanes(west[...], east[...], p, rows)
            rim_sides = side_lanes(rim[count], rim[count + 1], p, 2 * STEPS)
            field = widened(back[p], sides, rim[p], rim_sides)
            for _ in range(STEPS):
                carried = wide_diff[l] * field
                field = field + (neighbours(carried) - 4.0 * carried)
            out[p] = control[p] + field[:rows, :LANES]
        return carry

    lax.fori_loop(0, count // levels, one, 0)


def shape_of(*shape):
    return jax.ShapeDtypeStruct(shape, jnp.float32)


def rim_rows(planes, west, east):
    south = jnp.concatenate([p[:, :STEPS] for p in planes] + [west[None, :STEPS], east[None, :STEPS]], axis=0)
    north = jnp.concatenate([p[:, -STEPS:] for p in planes] + [west[None, -STEPS:], east[None, -STEPS:]], axis=0)
    from_north, from_south = exchange(north, south, "gy")
    return jnp.concatenate([from_south, from_north], axis=1)


def shards(control, perturb, obs_count, obs_weight, diffusivity):
    members, levels, rows, columns = control.shape
    variables = perturb.shape[1]
    ways = lax.axis_size("mem")
    scale = 1.0 / math.sqrt(members * ways - 1)
    count = members * levels
    flat = control.reshape(count, rows, columns)

    first, last = pl.pallas_call(
        pack_kernel, out_shape=(shape_of(rows, LANES), shape_of(rows, LANES)), name="pack"
    )(flat, diffusivity)
    west, east = exchange(last, first, "gx")
    rim = rim_rows([flat, diffusivity], west, east)

    partial, wide_diff = pl.pallas_call(
        lambda *refs: spread_kernel(levels, *refs),
        out_shape=(shape_of(variables * levels, rows, columns), shape_of(levels, rows + 2 * STEPS, 2 * LANES)),
        scratch_shapes=[pltpu.VMEM((count, rows, columns), jnp.float32)],
        name="spread",
    )(flat, diffusivity, west, east, rim, perturb)

    parts = lax.all_to_all(partial.reshape(ways, -1, columns), "mem", 0, 0)
    mine = jnp.sum(parts, axis=0)
    increment = lax.all_to_all(jnp.broadcast_to(mine, parts.shape), "mem", 0, 0)
    increment = increment.reshape(variables * levels, rows, columns)

    back, first, last = pl.pallas_call(
        lambda *refs: back_kernel(scale, *refs),
        out_shape=(shape_of(count, rows, columns), shape_of(rows, LANES), shape_of(rows, LANES)),
        in_specs=[
            pl.BlockSpec(memory_space=pltpu.VMEM),
            pl.BlockSpec(memory_space=pltpu.VMEM),
            pl.BlockSpec(memory_space=pltpu.SMEM),
            pl.BlockSpec(memory_space=pltpu.VMEM),
        ],
        scratch_shapes=[pltpu.VMEM((variables * levels, rows, columns), jnp.float32)],
        name="back",
    )(increment, obs_count, obs_weight, perturb)
    west, east = exchange(last, first, "gx")
    rim = rim_rows([back], west, east)

    out = pl.pallas_call(
        lambda *refs: adjoint_kernel(levels, *refs),
        out_shape=shape_of(count, rows, columns),
        name="adjoint",
    )(flat, back, wide_diff, west, east, rim)
    return out.reshape(control.shape)


def solution(mesh):
    placed = (
        P("mem", None, "gy", "gx"),
        P("mem", None, None, "gy", "gx"),
        P(None, "gy", "gx"),
        P(),
        P(None, "gy", "gx"),
    )
    return jax.shard_map(
        shards, mesh=mesh, in_specs=placed, out_specs=P("mem", None, "gy", "gx"), check_vma=False
    )
```

```python
import math

import jax
import jax.numpy as jnp
from jax import lax
from jax.experimental import pallas as pl
from jax.experimental.pallas import tpu as pltpu
from jax.sharding import PartitionSpec as P

STEPS = 4
LANES = 128
PARAMS = pltpu.CompilerParams(vmem_limit_bytes=16 << 20)


def swap(near, far, axis):
    size = lax.axis_size(axis)
    out = []
    for value, start in ((near, 0), (far, 1)):
        pairs = []
        for i in range(start, size - 1, 2):
            pairs += [(i, i + 1), (i + 1, i)]
        out.append(lax.ppermute(value, axis, pairs))
    return out


def is_odd(axis):
    return lax.rem(lax.axis_index(axis), 2) == 1


def ordered(odd, first, last):
    return jnp.where(odd, first, last), jnp.where(odd, last, first)


def lane_ids(rows):
    return lax.broadcasted_iota(jnp.int32, (rows, LANES), 1)


def send_rows(count, source, near, far):
    odd = is_odd("gy")
    for p in range(count):
        plane = source(p)
        rows = plane.shape[0]
        near[p], far[p] = ordered(odd, plane[:STEPS], plane[rows - STEPS :])


def rows_kernel(control, diffusivity, near, far):
    count = control.shape[0]
    levels = diffusivity.shape[0]
    send_rows(count + levels, lambda p: control[p] if p < count else diffusivity[p - count], near, far)


def columns_kernel(parts, *refs):
    arrays, (got_near, got_far, rim, near, far) = refs[:parts], refs[parts:]
    odd = is_odd("gy")
    planes = [(a, p) for a in arrays for p in range(a.shape[0])]
    rows = arrays[0].shape[1] + 2 * STEPS
    group = lane_ids(rows) // STEPS
    first = jnp.zeros((rows, LANES), jnp.float32)
    last = jnp.zeros((rows, LANES), jnp.float32)
    for p, (a, q) in enumerate(planes):
        after, before = ordered(odd, got_far[p], got_near[p])
        ring = jnp.concatenate([after, before], axis=0)
        rim[p] = ring
        plane = jnp.concatenate([a[q], ring], axis=0)
        first = jnp.where(group == p, pltpu.roll(plane, (STEPS * p) % LANES, 1), first)
        last = jnp.where(group == p, pltpu.roll(plane, (STEPS * p + STEPS) % LANES, 1), last)
    near[...], far[...] = ordered(is_odd("gx"), first, last)


def sides_of(near, far):
    east, west = ordered(is_odd("gx"), far[...], near[...])
    return west, east


def widened(main, rim, west, east, p):
    lane = lane_ids(west.shape[0])
    east_part = pltpu.roll(east, lax.rem(2 * LANES - STEPS * p, LANES), 1)
    west_part = pltpu.roll(west, lax.rem(2 * LANES - STEPS - STEPS * p, LANES), 1)
    side = jnp.where(lane < STEPS, east_part, jnp.where(lane >= LANES - STEPS, west_part, 0.0))
    return jnp.concatenate([jnp.concatenate([main, rim], axis=0), side], axis=1)


def neighbours(field):
    rows, lanes = field.shape
    return (
        pltpu.roll(field, 1, 0)
        + pltpu.roll(field, rows - 1, 0)
        + pltpu.roll(field, 1, 1)
        + pltpu.roll(field, lanes - 1, 1)
    )


def spread_kernel(control, diffusivity, rim, near, far, perturb_hbm, partial, wide_diff, spread, perturb, sem):
    copy = pltpu.make_async_copy(perturb_hbm, perturb, sem)
    copy.start()
    count, rows, _ = control.shape
    levels = diffusivity.shape[0]
    members = count // levels
    variables = perturb.shape[1]
    west, east = sides_of(near, far)
    for l in range(levels):
        wide_diff[l] = widened(diffusivity[l], rim[count + l], west, east, count + l)

    def one(m, carry):
        for l in range(levels):
            p = m * levels + l
            field = widened(control[p], rim[p], west, east, p)
            for _ in range(STEPS):
                field = field + wide_diff[l] * (neighbours(field) - 4.0 * field)
            spread[p] = field[:rows, :LANES]
        return carry

    lax.fori_loop(0, members, one, 0)
    copy.wait()
    for v in range(variables):
        for l in range(levels):
            total = perturb[0, v, l].astype(jnp.float32) * spread[l]
            for m in range(1, members):
                total = total + perturb[m, v, l].astype(jnp.float32) * spread[m * levels + l]
            partial[v * levels + l] = total


def back_kernel(scale, increment, obs_count, obs_weight, perturb, back, near, far, weighted):
    members, variables, levels, rows, _ = perturb.shape
    for l in range(levels):
        seen = obs_count[l].astype(jnp.float32) * (scale * scale)
        for v in range(variables):
            weighted[v * levels + l] = seen * obs_weight[v] * increment[v * levels + l]
    for m in range(members):
        for l in range(levels):
            total = perturb[m, 0, l].astype(jnp.float32) * weighted[l]
            for v in range(1, variables):
                total = total + perturb[m, v, l].astype(jnp.float32) * weighted[v * levels + l]
            back[m * levels + l] = total
    send_rows(members * levels, lambda p: back[p], near, far)


def adjoint_kernel(control, back, wide_diff, rim, near, far, out):
    count, rows, _ = back.shape
    levels = wide_diff.shape[0]
    west, east = sides_of(near, far)

    def one(m, carry):
        for l in range(levels):
            p = m * levels + l
            field = widened(back[p], rim[p], west, east, p)
            for _ in range(STEPS):
                carried = wide_diff[l] * field
                field = field + (neighbours(carried) - 4.0 * carried)
            out[p] = control[p] + field[:rows, :LANES]
        return carry

    lax.fori_loop(0, count // levels, one, 0)


def shape_of(*shape):
    return jax.ShapeDtypeStruct(shape, jnp.float32)


def columns(*arrays, rows):
    total = sum(a.shape[0] for a in arrays)
    ring = arrays[0].shape[1] + 2 * STEPS
    near, far = rows
    rim, near, far = pl.pallas_call(
        lambda *refs: columns_kernel(len(arrays), *refs),
        out_shape=(shape_of(total, 2 * STEPS, LANES), shape_of(ring, LANES), shape_of(ring, LANES)),
        compiler_params=PARAMS,
        name="columns",
    )(*arrays, near, far)
    return rim, *swap(near, far, "gx")


def shards(control, perturb, obs_count, obs_weight, diffusivity):
    members, levels, rows, lanes = control.shape
    variables = perturb.shape[1]
    ways = lax.axis_size("mem")
    scale = 1.0 / math.sqrt(members * ways - 1)
    count = members * levels
    ring = rows + 2 * STEPS
    flat = control.reshape(count, rows, lanes)
    vmem = pl.BlockSpec(memory_space=pltpu.VMEM)

    edge = shape_of(count + levels, STEPS, lanes)
    near, far = pl.pallas_call(rows_kernel, out_shape=(edge, edge), compiler_params=PARAMS, name="rows")(flat, diffusivity)
    rim, near, far = columns(flat, diffusivity, rows=swap(near, far, "gy"))

    partial, wide_diff = pl.pallas_call(
        spread_kernel,
        out_shape=(shape_of(variables * levels, rows, lanes), shape_of(levels, ring, 2 * lanes)),
        in_specs=[vmem] * 5 + [pl.BlockSpec(memory_space=pltpu.HBM)],
        scratch_shapes=[
            pltpu.VMEM((count, rows, lanes), jnp.float32),
            pltpu.VMEM(perturb.shape, perturb.dtype),
            pltpu.SemaphoreType.DMA,
        ],
        compiler_params=PARAMS,
        name="spread",
    )(flat, diffusivity, rim, near, far, pltpu.with_memory_space_constraint(perturb, pltpu.HBM))

    parts = lax.all_to_all(partial.reshape(ways, -1, lanes), "mem", 0, 0)
    mine = jnp.sum(parts, axis=0)
    increment = lax.all_to_all(jnp.broadcast_to(mine, parts.shape), "mem", 0, 0)
    increment = increment.reshape(variables * levels, rows, lanes)

    edge = shape_of(count, STEPS, lanes)
    back, near, far = pl.pallas_call(
        lambda *refs: back_kernel(scale, *refs),
        out_shape=(shape_of(count, rows, lanes), edge, edge),
        in_specs=[vmem, vmem, pl.BlockSpec(memory_space=pltpu.SMEM), vmem],
        scratch_shapes=[pltpu.VMEM((variables * levels, rows, lanes), jnp.float32)],
        compiler_params=PARAMS,
        name="back",
    )(increment, obs_count, obs_weight, perturb)
    rim, near, far = columns(back, rows=swap(near, far, "gy"))

    out = pl.pallas_call(adjoint_kernel, out_shape=shape_of(count, rows, lanes), compiler_params=PARAMS, name="adjoint")(
        flat, back, wide_diff, rim, near, far
    )
    return out.reshape(control.shape)


def solution(mesh):
    placed = (
        P("mem", None, "gy", "gx"),
        P("mem", None, None, "gy", "gx"),
        P(None, "gy", "gx"),
        P(),
        P(None, "gy", "gx"),
    )
    return jax.shard_map(
        shards, mesh=mesh, in_specs=placed, out_specs=P("mem", None, "gy", "gx"), check_vma=False
    )
```

```python
import math

import jax
import jax.numpy as jnp
from jax import lax
from jax.experimental import pallas as pl
from jax.experimental.pallas import tpu as pltpu
from jax.sharding import PartitionSpec as P

STEPS = 4
LANES = 128
SUBLANES = 8
PARAMS = pltpu.CompilerParams(vmem_limit_bytes=16 << 20)


def swap(near, far, axis):
    size = lax.axis_size(axis)
    out = []
    for value, start in ((near, 0), (far, 1)):
        pairs = []
        for i in range(start, size - 1, 2):
            pairs += [(i, i + 1), (i + 1, i)]
        out.append(lax.ppermute(value, axis, pairs))
    return out


def is_odd(axis):
    return lax.rem(lax.axis_index(axis), 2) == 1


def ordered(odd, first, last):
    return jnp.where(odd, first, last), jnp.where(odd, last, first)


class Grid:
    def __init__(self, members, levels, rows):
        self.members, self.levels, self.rows = members, levels, rows
        self.ring = rows + 2 * STEPS
        self.block = LANES // levels // STEPS * STEPS
        self.per = self.block // STEPS
        self.packs = -(-self.ring // self.per)

    def members_at(self, level, y):
        return pl.ds(level * self.rows + y, self.members, stride=self.levels * self.rows)

    def ring_row(self, field, got, odd, level, k):
        y = k - STEPS
        if 0 <= y < self.rows:
            return field[self.members_at(level, y), :]
        before = y < 0
        at = level * STEPS + (k if before else y - self.rows)
        near, far = got
        after_value, before_value = ordered(odd, far[at], near[at])
        return before_value if before else after_value

    def lanes(self, rows=SUBLANES):
        lane = lax.broadcasted_iota(jnp.int32, (rows, LANES), 1)
        return lax.rem(lane, self.block)


def within(place, start, size):
    return (place >= start) & (place < start + size)


def rolled(value, shift):
    shift %= LANES
    return pltpu.roll(value, shift, 1) if shift else value


def edges_of(grid, value_of, rows=SUBLANES):
    lane = lax.broadcasted_iota(jnp.int32, (rows, LANES), 1)
    out = jnp.zeros((rows, LANES), jnp.float32)
    for l in range(grid.levels):
        base = l * grid.block
        out = jnp.where(within(lane, base, 4 * STEPS), rolled(value_of(l), base + 2 * STEPS), out)
    return out


def packed(grid, edges, rows=SUBLANES):
    place = grid.lanes(rows)
    first = jnp.zeros((rows, LANES), jnp.float32)
    last = first
    for i, value in enumerate(edges):
        mask = within(place, i * STEPS, STEPS)
        first = jnp.where(mask, rolled(value, (i - 2) * STEPS), first)
        last = jnp.where(mask, rolled(value, (i - 1) * STEPS), last)
    return first, last


def strip_of(grid, edges, west, east, i, rows=SUBLANES):
    place = grid.lanes(rows)
    out = jnp.where(place < 2 * STEPS, edges, 0.0)
    out = jnp.where(within(place, 6 * STEPS, 2 * STEPS), rolled(edges, 4 * STEPS), out)
    out = jnp.where(within(place, 2 * STEPS, STEPS), rolled(east, (2 - i) * STEPS), out)
    return jnp.where(within(place, 5 * STEPS, STEPS), rolled(west, (5 - i) * STEPS), out)


def joined(grid, strip):
    return jnp.where(grid.lanes() < 2 * STEPS, strip, rolled(strip, -4 * STEPS))


def merged(grid, main, ends, level):
    lane = lax.broadcasted_iota(jnp.int32, (SUBLANES, LANES), 1)
    outer = (lane < STEPS) | (lane >= LANES - STEPS)
    return jnp.where(outer, rolled(ends, LANES - 2 * STEPS - level * grid.block), main)


def lateral(value):
    return pltpu.roll(value, 1, 1) + pltpu.roll(value, LANES - 1, 1)


def spread_steps(field, coef, keep):
    for s in range(1, STEPS + 1):
        new = list(field)
        for k in range(s, len(field) - s):
            around = (field[k - 1] + field[k + 1]) + lateral(field[k])
            new[k] = keep(k) * field[k] + coef(k) * around
        field = new
    return field[STEPS:-STEPS]


def adjoint_steps(field, coef, keep):
    for s in range(1, STEPS + 1):
        flux = {k: coef(k) * field[k] for k in range(s - 1, len(field) - s + 1)}
        new = list(field)
        for k in range(s, len(field) - s):
            new[k] = keep(k) * field[k] + ((flux[k - 1] + flux[k + 1]) + lateral(flux[k]))
        field = new
    return field[STEPS:-STEPS]


def row_reader(ref, start):
    return lambda k: jnp.broadcast_to(ref[pl.ds(start + k, 1), :], (SUBLANES, LANES))


def rows_kernel(grid, control_hbm, diffusivity_hbm, near, far, control, diffusivity, sems):
    levels, rows = grid.levels, grid.rows
    copies = [
        pltpu.make_async_copy(diffusivity_hbm, diffusivity, sems.at[0]),
        pltpu.make_async_copy(control_hbm, control, sems.at[1]),
    ]
    for copy in copies:
        copy.start()
    odd = is_odd("gy")
    copies[0].wait()
    for l in range(levels):
        first = diffusivity[l * rows : l * rows + STEPS, :]
        last = diffusivity[(l + 1) * rows - STEPS : (l + 1) * rows, :]
        slot, at = divmod(l * STEPS, SUBLANES)
        a, b = ordered(odd, first, last)
        near[levels * STEPS + slot, at : at + STEPS, :] = a
        far[levels * STEPS + slot, at : at + STEPS, :] = b
    copies[1].wait()
    send_rows(grid, control, near, far)


def send_rows(grid, field, near, far):
    odd = is_odd("gy")
    for l in range(grid.levels):
        for r in range(STEPS):
            first = field[grid.members_at(l, r), :]
            last = field[grid.members_at(l, grid.rows - STEPS + r), :]
            near[l * STEPS + r], far[l * STEPS + r] = ordered(odd, first, last)


def field_columns(grid, field, got, near, far, edges):
    odd = is_odd("gy")
    for q in range(grid.packs):
        here = []
        for k in range(q * grid.per, min(grid.ring, (q + 1) * grid.per)):
            here.append(edges_of(grid, lambda l: grid.ring_row(field, got, odd, l, k)))
            edges[k] = here[-1]
        near[q], far[q] = ordered(is_odd("gx"), *packed(grid, here))


def columns_kernel(grid, control, diffusivity, got_near, got_far, near, far, edges, ring, ring_edges):
    got = (got_near, got_far)
    field_columns(grid, control, got, near, far, edges)
    odd = is_odd("gy")
    for l in range(grid.levels):
        slot, at = divmod(l * STEPS, SUBLANES)
        from_near, from_far = (g[grid.levels * STEPS + slot, at : at + STEPS, :] for g in got)
        after, before = ordered(odd, from_far, from_near)
        base = l * grid.ring
        ring[base : base + STEPS, :] = before
        ring[base + STEPS : base + STEPS + grid.rows, :] = diffusivity[l * grid.rows : (l + 1) * grid.rows, :]
        ring[base + STEPS + grid.rows : base + grid.ring, :] = after
    ring_edges[...] = edges_of(grid, lambda l: ring[l * grid.ring : (l + 1) * grid.ring, :], grid.ring)
    spaced = [ring_edges[pl.ds(i, grid.packs, stride=grid.per), :] for i in range(grid.per)]
    a, b = ordered(is_odd("gx"), *packed(grid, spaced, grid.packs))
    near[grid.packs, : grid.packs, :] = a
    far[grid.packs, : grid.packs, :] = b


def back_columns_kernel(grid, back, got_near, got_far, near, far, edges):
    field_columns(grid, back, (got_near, got_far), near, far, edges)


def main_steps(grid, steps, field, ring, got, keep, out):
    odd = is_odd("gy")
    keep[...] = 1.0 - 4.0 * ring[...]
    for l in range(grid.levels):
        rows = [grid.ring_row(field, got, odd, l, k) for k in range(grid.ring)]
        for y, row in enumerate(steps(rows, row_reader(ring, l * grid.ring), row_reader(keep, l * grid.ring))):
            out[l * grid.rows + y] = row


def spread_main_kernel(grid, control, ring, got_near, got_far, perturb_hbm, main, perturb, keep, sem):
    copy = pltpu.make_async_copy(perturb_hbm, perturb, sem)
    copy.start()
    main_steps(grid, spread_steps, control, ring, (got_near, got_far), keep, main)
    copy.wait()


def adjoint_main_kernel(grid, back, ring, got_near, got_far, main, keep):
    main_steps(grid, adjoint_steps, back, ring, (got_near, got_far), keep, main)


def sides(col_near, col_far, q):
    east, west = ordered(is_odd("gx"), col_far[q], col_near[q])
    return west, east


def strip_steps(grid, steps, edges, col_near, col_far, strip_ring, strip_keep, ends):
    strip_keep[...] = 1.0 - 4.0 * strip_ring[...]
    field = []
    for k in range(grid.ring):
        q, i = divmod(k, grid.per)
        field.append(strip_of(grid, edges[k], *sides(col_near, col_far, q), i))
    for y, strip in enumerate(steps(field, row_reader(strip_ring, 0), row_reader(strip_keep, 0))):
        ends[y] = joined(grid, strip)


def spread_kernel(grid, main, edges, ring_edges, col_near, col_far, perturb, partial, strip_ring, strip_keep, ends, spread):
    west, east = (side[: grid.packs] for side in sides(col_near, col_far, grid.packs))
    for i in range(grid.per):
        at = pl.ds(i, grid.packs, stride=grid.per)
        strip_ring[at, :] = strip_of(grid, ring_edges[at, :], west, east, i, grid.packs)
    strip_steps(grid, spread_steps, edges, col_near, col_far, strip_ring, strip_keep, ends)
    members, variables, levels, rows, _ = perturb.shape
    for l in range(levels):
        for y in range(rows):
            spread[grid.members_at(l, y), :] = merged(grid, main[l * rows + y], ends[y], l)
    tile = 2 * SUBLANES
    for l in range(levels):
        for start in range(0, rows, tile):
            here = [spread[(m * levels + l) * rows + start : (m * levels + l) * rows + start + tile, :] for m in range(members)]
            for v in range(variables):
                total = perturb[0, v, l, start : start + tile, :].astype(jnp.float32) * here[0]
                for m in range(1, members):
                    total = total + perturb[m, v, l, start : start + tile, :].astype(jnp.float32) * here[m]
                partial[v * levels + l, start : start + tile, :] = total


def back_kernel(grid, scale, increment, obs_count, obs_weight, perturb, back, near, far):
    members, variables, levels, rows, _ = perturb.shape
    tile = 2 * SUBLANES
    for l in range(levels):
        for start in range(0, rows, tile):
            at = slice(start, start + tile)
            seen = obs_count[l, at, :].astype(jnp.float32) * (scale * scale)
            weighted = [seen * obs_weight[v] * increment[v * levels + l, at, :] for v in range(variables)]
            for m in range(members):
                total = perturb[m, 0, l, at, :].astype(jnp.float32) * weighted[0]
                for v in range(1, variables):
                    total = total + perturb[m, v, l, at, :].astype(jnp.float32) * weighted[v]
                base = (m * levels + l) * rows
                back[base + start : base + start + tile, :] = total
    send_rows(grid, back, near, far)


def adjoint_kernel(grid, control, main, edges, strip_ring, col_near, col_far, out, strip_keep, ends):
    strip_steps(grid, adjoint_steps, edges, col_near, col_far, strip_ring, strip_keep, ends)
    for l in range(grid.levels):
        for y in range(grid.rows):
            at = grid.members_at(l, y)
            out[at, :] = control[at, :] + merged(grid, main[l * grid.rows + y], ends[y], l)


def shape_of(*shape):
    return jax.ShapeDtypeStruct(shape, jnp.float32)


def shards(control, perturb, obs_count, obs_weight, diffusivity):
    members, levels, rows, lanes = control.shape
    variables = perturb.shape[1]
    ways = lax.axis_size("mem")
    scale = 1.0 / math.sqrt(members * ways - 1)
    count = members * levels
    grid = Grid(members, levels, rows)
    assert members == SUBLANES and lanes == LANES and grid.block >= 8 * STEPS
    vmem = pl.BlockSpec(memory_space=pltpu.VMEM)
    hbm = pl.BlockSpec(memory_space=pltpu.HBM)
    f32 = jnp.float32

    def call(kernel, name, *args, work=0, **kwargs):
        cost = pl.CostEstimate(flops=work, bytes_accessed=work, transcendentals=0) if work else None
        return pl.pallas_call(lambda *refs: kernel(grid, *refs), name=name, compiler_params=PARAMS, cost_estimate=cost, **kwargs)(*args)

    def in_hbm(array):
        return pltpu.with_memory_space_constraint(array, pltpu.HBM)

    ring_shape, strip_shape = (levels * grid.ring, lanes), (grid.ring, lanes)
    edges_shape = shape_of(grid.ring, SUBLANES, lanes)
    main_shape = shape_of(levels * rows, SUBLANES, lanes)
    edge = shape_of(levels * STEPS + -(-levels * STEPS // SUBLANES), SUBLANES, lanes)
    near, far, flat, flat_diff = call(
        rows_kernel,
        "rows",
        in_hbm(control.reshape(count * rows, lanes)),
        in_hbm(diffusivity.reshape(levels * rows, lanes)),
        out_shape=(edge, edge, shape_of(count * rows, lanes), shape_of(levels * rows, lanes)),
        in_specs=[hbm, hbm],
        scratch_shapes=[pltpu.SemaphoreType.DMA((2,))],
    )
    got = swap(near, far, "gy")
    edge = shape_of(grid.packs + 1, SUBLANES, lanes)
    near, far, edges, ring, ring_edges = call(
        columns_kernel,
        "columns",
        flat,
        flat_diff,
        *got,
        out_shape=(edge, edge, edges_shape, shape_of(*ring_shape), shape_of(*strip_shape)),
    )
    sides = swap(near, far, "gx")
    main, held = call(
        spread_main_kernel,
        "spread_main",
        flat,
        ring,
        *got,
        in_hbm(perturb),
        work=6 << 20,
        out_shape=(main_shape, jax.ShapeDtypeStruct(perturb.shape, perturb.dtype)),
        in_specs=[vmem] * 4 + [hbm],
        scratch_shapes=[pltpu.VMEM(ring_shape, f32), pltpu.SemaphoreType.DMA],
    )
    partial, strip_ring = call(
        spread_kernel,
        "spread",
        main,
        edges,
        ring_edges,
        *sides,
        held,
        out_shape=(shape_of(variables * levels, rows, lanes), shape_of(*strip_shape)),
        scratch_shapes=[
            pltpu.VMEM(strip_shape, f32),
            pltpu.VMEM((rows, SUBLANES, lanes), f32),
            pltpu.VMEM((count * rows, lanes), f32),
        ],
    )

    parts = lax.all_to_all(partial.reshape(ways, -1, lanes), "mem", 0, 0)
    mine = jnp.sum(parts, axis=0)
    increment = lax.all_to_all(jnp.broadcast_to(mine, parts.shape), "mem", 0, 0)
    increment = increment.reshape(variables * levels, rows, lanes)

    edge = shape_of(levels * STEPS, SUBLANES, lanes)
    back, near, far = call(
        lambda grid, *refs: back_kernel(grid, scale, *refs),
        "back",
        increment,
        obs_count,
        obs_weight,
        held,
        out_shape=(shape_of(count * rows, lanes), edge, edge),
        in_specs=[vmem, vmem, pl.BlockSpec(memory_space=pltpu.SMEM), vmem],
    )
    got = swap(near, far, "gy")
    edge = shape_of(grid.packs, SUBLANES, lanes)
    near, far, edges = call(back_columns_kernel, "back_columns", back, *got, out_shape=(edge, edge, edges_shape))
    sides = swap(near, far, "gx")
    main = call(
        adjoint_main_kernel,
        "adjoint_main",
        back,
        ring,
        *got,
        work=6 << 20,
        out_shape=main_shape,
        scratch_shapes=[pltpu.VMEM(ring_shape, f32)],
    )
    out = call(
        adjoint_kernel,
        "adjoint",
        flat,
        main,
        edges,
        strip_ring,
        *sides,
        out_shape=shape_of(count * rows, lanes),
        scratch_shapes=[pltpu.VMEM(strip_shape, f32), pltpu.VMEM((rows, SUBLANES, lanes), f32)],
    )
    return out.reshape(control.shape)


def solution(mesh):
    placed = (
        P("mem", None, "gy", "gx"),
        P("mem", None, None, "gy", "gx"),
        P(None, "gy", "gx"),
        P(),
        P(None, "gy", "gx"),
    )
    return jax.shard_map(
        shards, mesh=mesh, in_specs=placed, out_specs=P("mem", None, "gy", "gx"), check_vma=False
    )
```

```python
import math

import jax
import jax.numpy as jnp
from jax import lax
from jax.experimental import pallas as pl
from jax.experimental.pallas import tpu as pltpu
from jax.sharding import PartitionSpec as P


STEPS = 4
LANES = 128
SUBLANES = 8
PARAMS = pltpu.CompilerParams(vmem_limit_bytes=16 << 20)


def swap(near, far, axis):
    size = lax.axis_size(axis)
    out = []
    for value, start in ((near, 0), (far, 1)):
        pairs = []
        for i in range(start, size - 1, 2):
            pairs += [(i, i + 1), (i + 1, i)]
        out.append(lax.ppermute(value, axis, pairs))
    return out


def is_odd(axis):
    return lax.rem(lax.axis_index(axis), 2) == 1


def ordered(odd, first, last):
    return jnp.where(odd, first, last), jnp.where(odd, last, first)


class Grid:
    def __init__(self, members, levels, rows):
        self.members, self.levels, self.rows = members, levels, rows
        self.wide = rows + 4 * STEPS
        self.ring = rows + 2 * STEPS
        self.block = LANES // levels // STEPS * STEPS
        self.per = self.block // STEPS
        self.wide_packs = -(-self.wide // self.per)
        self.packs = -(-self.ring // self.per)
        self.padded = -(-self.wide_packs * self.per // SUBLANES) * SUBLANES

    def members_at(self, level, y):
        return pl.ds(level * self.rows + y, self.members, stride=self.levels * self.rows)

    def rim_at(self, level, r):
        return pl.ds(level * self.members * STEPS + r, self.members, stride=STEPS)

    def wide_row(self, field, got, odd, level, k):
        y = k - 2 * STEPS
        if 0 <= y < self.rows:
            return field[self.members_at(level, y), :]
        before = y < 0
        at = level * 2 * STEPS + (k if before else y - self.rows)
        near, far = got
        after_value, before_value = ordered(odd, far[at], near[at])
        return before_value if before else after_value

    def ring_row(self, field, before, after, level, k):
        y = k - STEPS
        if y < 0:
            return before[self.rim_at(level, k), :]
        if y >= self.rows:
            return after[self.rim_at(level, y - self.rows), :]
        return field[self.members_at(level, y), :]

    def tile_of(self, ref, plane, j):
        t = plane * (self.ring // SUBLANES) + j
        return t // (ref.shape[1] // SUBLANES), pl.ds(t % (ref.shape[1] // SUBLANES) * SUBLANES, SUBLANES)

    def lanes(self, rows=SUBLANES):
        lane = lax.broadcasted_iota(jnp.int32, (rows, LANES), 1)
        return lax.rem(lane, self.block)


def within(place, start, size):
    return (place >= start) & (place < start + size)


def rolled(value, shift):
    shift %= LANES
    return pltpu.roll(value, shift, 1) if shift else value


def edges_of(grid, value_of, rows=SUBLANES):
    lane = lax.broadcasted_iota(jnp.int32, (rows, LANES), 1)
    out = jnp.zeros((rows, LANES), jnp.float32)
    for l in range(grid.levels):
        base = l * grid.block
        out = jnp.where(within(lane, base, 4 * STEPS), rolled(value_of(l), base + 2 * STEPS), out)
    return out


def packed(grid, edges, rows=SUBLANES):
    place = grid.lanes(rows)
    first = jnp.zeros((rows, LANES), jnp.float32)
    last = first
    for i, value in enumerate(edges):
        mask = within(place, i * STEPS, STEPS)
        first = jnp.where(mask, rolled(value, (i - 2) * STEPS), first)
        last = jnp.where(mask, rolled(value, (i - 1) * STEPS), last)
    return first, last


def strip_of(grid, edges, west, east, i, rows=SUBLANES):
    place = grid.lanes(rows)
    out = jnp.where(place < 2 * STEPS, edges, 0.0)
    out = jnp.where(within(place, 6 * STEPS, 2 * STEPS), rolled(edges, 4 * STEPS), out)
    out = jnp.where(within(place, 2 * STEPS, STEPS), rolled(east, (2 - i) * STEPS), out)
    return jnp.where(within(place, 5 * STEPS, STEPS), rolled(west, (5 - i) * STEPS), out)


def joined(grid, strip):
    return jnp.where(grid.lanes() < 2 * STEPS, strip, rolled(strip, -4 * STEPS))


def merged(grid, main, ends, level):
    lane = lax.broadcasted_iota(jnp.int32, (SUBLANES, LANES), 1)
    outer = (lane < STEPS) | (lane >= LANES - STEPS)
    return jnp.where(outer, rolled(ends, LANES - 2 * STEPS - level * grid.block), main)


def lateral(value):
    return pltpu.roll(value, 1, 1) + pltpu.roll(value, LANES - 1, 1)


def spread_steps(field, coef, keep):
    for s in range(1, STEPS + 1):
        new = list(field)
        for k in range(s, len(field) - s):
            around = (field[k - 1] + field[k + 1]) + lateral(field[k])
            new[k] = keep(k) * field[k] + coef(k) * around
        field = new
    return field[STEPS:-STEPS]


def adjoint_steps(field, coef, keep):
    for s in range(1, STEPS + 1):
        flux = {k: coef(k) * field[k] for k in range(s - 1, len(field) - s + 1)}
        new = list(field)
        for k in range(s, len(field) - s):
            new[k] = keep(k) * field[k] + ((flux[k - 1] + flux[k + 1]) + lateral(flux[k]))
        field = new
    return field[STEPS:-STEPS]


def row_reader(ref, start):
    return lambda k: jnp.broadcast_to(ref[pl.ds(start + k, 1), :], (SUBLANES, LANES))


def rows_kernel(grid, control_hbm, diffusivity_hbm, count_hbm, near, far, control, diffusivity, seen, count, sems):
    levels, rows = grid.levels, grid.rows
    depth = 2 * STEPS
    copies = [
        pltpu.make_async_copy(diffusivity_hbm, diffusivity, sems.at[0]),
        pltpu.make_async_copy(count_hbm, count, sems.at[1]),
        pltpu.make_async_copy(control_hbm, control, sems.at[2]),
    ]
    for copy in copies:
        copy.start()
    odd = is_odd("gy")
    copies[0].wait()
    copies[1].wait()
    seen[...] = count[...].astype(jnp.float32)
    at = levels * depth
    for l in range(levels):
        first = diffusivity[l * rows : l * rows + depth, :]
        last = diffusivity[(l + 1) * rows - depth : (l + 1) * rows, :]
        near[at + l], far[at + l] = ordered(odd, first, last)
        first = seen[l * rows : l * rows + STEPS, :]
        last = seen[(l + 1) * rows - STEPS : (l + 1) * rows, :]
        slot, sub = divmod(l * STEPS, SUBLANES)
        a, b = ordered(odd, first, last)
        near[at + levels + slot, sub : sub + STEPS, :] = a
        far[at + levels + slot, sub : sub + STEPS, :] = b
    copies[2].wait()
    for l in range(levels):
        for r in range(depth):
            first = control[grid.members_at(l, r), :]
            last = control[grid.members_at(l, rows - depth + r), :]
            near[l * depth + r], far[l * depth + r] = ordered(odd, first, last)


def turned(value):
    return pltpu.roll(value, STEPS, 0)


def upper():
    return lax.broadcasted_iota(jnp.int32, (SUBLANES, LANES), 0) < STEPS


def perturb_rows_kernel(grid, order, perturb_hbm, near, far, perturb, sems):
    members, variables, levels, rows, _ = perturb.shape
    copies = [
        pltpu.make_async_copy(perturb_hbm.at[pl.ds(2 * q, 2)], perturb.at[pl.ds(2 * q, 2)], sems.at[q]) for q in range(members // 2)
    ]
    for copy in copies:
        copy.start()
    odd = is_odd("gy")
    tile = 2 * SUBLANES
    for q, copy in enumerate(copies):
        copy.wait()
        for v in range(variables):
            for l in range(levels):
                heads = [perturb[2 * q + j, v, l, :tile, :].astype(jnp.float32)[:SUBLANES] for j in range(2)]
                tails = [perturb[2 * q + j, v, l, rows - tile :, :].astype(jnp.float32)[SUBLANES:] for j in range(2)]
                first = jnp.where(upper(), heads[0], turned(heads[1]))
                last = jnp.where(upper(), turned(tails[0]), tails[1])
                at = (v * levels + l) * (members // 2) + q
                near[at], far[at] = ordered(odd, first, last)


def field_columns(grid, row_of, length, near, far, edges):
    for start in range(0, length, grid.per):
        here = []
        for k in range(start, min(length, start + grid.per)):
            here.append(edges_of(grid, lambda l: row_of(l, k)))
            edges[k] = here[-1]
        q = start // grid.per
        near[q], far[q] = ordered(is_odd("gx"), *packed(grid, here))


def columns_kernel(grid, control, diffusivity, got_near, got_far, near, far, edges, ring, ring_edges):
    got = (got_near, got_far)
    odd = is_odd("gy")
    field_columns(grid, lambda l, k: grid.wide_row(control, got, odd, l, k), grid.wide, near, far, edges)
    depth = 2 * STEPS
    for l in range(grid.levels):
        after, before = ordered(odd, got_far[grid.levels * depth + l], got_near[grid.levels * depth + l])
        base = l * grid.wide
        ring[base : base + depth, :] = before
        ring[base + depth : base + depth + grid.rows, :] = diffusivity[l * grid.rows : (l + 1) * grid.rows, :]
        ring[base + depth + grid.rows : base + grid.wide, :] = after
    ring_edges[...] = jnp.zeros(ring_edges.shape, jnp.float32)
    ring_edges[: grid.wide, :] = edges_of(grid, lambda l: ring[l * grid.wide : (l + 1) * grid.wide, :], grid.wide)
    packs = grid.wide_packs
    spaced = [ring_edges[pl.ds(i, packs, stride=grid.per), :] for i in range(grid.per)]
    a, b = ordered(is_odd("gx"), *packed(grid, spaced, packs))
    near[packs, :packs, :] = a
    far[packs, :packs, :] = b


def spread_main_kernel(grid, control, ring, got_near, got_far, main, keep):
    odd = is_odd("gy")
    keep[...] = 1.0 - 4.0 * ring[...]
    for l in range(grid.levels):
        rows = [grid.wide_row(control, (got_near, got_far), odd, l, k) for k in range(grid.wide)]
        at = l * grid.wide
        for y, row in enumerate(spread_steps(rows, row_reader(ring, at), row_reader(keep, at))):
            main[l * grid.ring + y] = row


def adjoint_main_kernel(grid, back, before, after, ring, main, keep):
    keep[...] = 1.0 - 4.0 * ring[...]
    for l in range(grid.levels):
        rows = [grid.ring_row(back, before, after, l, k) for k in range(grid.ring)]
        at = l * grid.wide + STEPS
        for y, row in enumerate(adjoint_steps(rows, row_reader(ring, at), row_reader(keep, at))):
            main[l * grid.rows + y] = row


def sides(col_near, col_far, q):
    east, west = ordered(is_odd("gx"), col_far[q], col_near[q])
    return west, east


def strip_steps(grid, steps, edges, length, skip, col_near, col_far, strip_ring, strip_keep, ends):
    strip_keep[...] = 1.0 - 4.0 * strip_ring[...]
    field = []
    for k in range(length):
        q, i = divmod(k, grid.per)
        field.append(strip_of(grid, edges[k], *sides(col_near, col_far, q), i))
    for y, strip in enumerate(steps(field, row_reader(strip_ring, skip), row_reader(strip_keep, skip))):
        ends[y] = joined(grid, strip)


def spread_kernel(
    grid,
    main,
    edges,
    ring_edges,
    col_near,
    col_far,
    perturb,
    rim_near,
    rim_far,
    partial,
    strip_ring,
    strip_keep,
    ends,
    spread,
    spread_before,
    spread_after,
):
    packs = grid.wide_packs
    west, east = (side[:packs] for side in sides(col_near, col_far, packs))
    strip_ring[...] = jnp.zeros(strip_ring.shape, jnp.float32)
    for i in range(grid.per):
        at = pl.ds(i, packs, stride=grid.per)
        strip_ring[at, :] = strip_of(grid, ring_edges[at, :], west, east, i, packs)
    strip_steps(grid, spread_steps, edges, grid.wide, 0, col_near, col_far, strip_ring, strip_keep, ends)
    members, variables, levels, rows, _ = perturb.shape
    for l in range(levels):
        for j in range(grid.ring):
            value = merged(grid, main[l * grid.ring + j], ends[j], l)
            y = j - STEPS
            if y < 0:
                spread_before[grid.rim_at(l, j), :] = value
            elif y >= rows:
                spread_after[grid.rim_at(l, y - rows), :] = value
            else:
                spread[grid.members_at(l, y), :] = value
    tile = 2 * SUBLANES
    odd = is_odd("gy")
    pairs = members // 2
    for l in range(levels):
        for start in range(0, rows, tile):
            here = [spread[(m * levels + l) * rows + start : (m * levels + l) * rows + start + tile, :] for m in range(members)]
            for v in range(variables):
                total = perturb[0, v, l, start : start + tile, :].astype(jnp.float32) * here[0]
                for m in range(1, members):
                    total = total + perturb[m, v, l, start : start + tile, :].astype(jnp.float32) * here[m]
                for j in range(2):
                    partial[grid.tile_of(partial, v * levels + l, start // SUBLANES + j)] = total[j * SUBLANES : (j + 1) * SUBLANES]
        rims = [(after, before) for after, before in zip(
            [spread_after[(l * pairs + q) * SUBLANES : (l * pairs + q + 1) * SUBLANES, :] for q in range(pairs)],
            [spread_before[(l * pairs + q) * SUBLANES : (l * pairs + q + 1) * SUBLANES, :] for q in range(pairs)],
        )]
        for v in range(variables):
            totals = [0.0, 0.0]
            for q in range(pairs):
                at = (v * levels + l) * pairs + q
                outer = ordered(odd, rim_far[at], rim_near[at])
                totals = [t + p * r for t, p, r in zip(totals, outer, rims[q])]
            after, before = (t + turned(t) for t in totals)
            partial[grid.tile_of(partial, v * levels + l, rows // SUBLANES)] = jnp.where(upper(), after, before)
    used = variables * levels * (grid.ring // SUBLANES)
    for t in range(used, partial.shape[0] * partial.shape[1] // SUBLANES):
        partial[grid.tile_of(partial, 0, t)] = jnp.zeros((SUBLANES, LANES), jnp.float32)


def back_kernel(
    grid,
    scale,
    increment,
    seen,
    obs_weight,
    perturb,
    rim_near,
    rim_far,
    got_near,
    got_far,
    back,
    back_before,
    back_after,
    edges,
    near,
    far,
):
    members, variables, levels, rows, _ = perturb.shape
    tile = 2 * SUBLANES
    odd = is_odd("gy")
    pairs = members // 2
    for l in range(levels):
        for start in range(0, rows, tile):
            factor = seen[l * rows + start : l * rows + start + tile, :] * (scale * scale)
            weighted = []
            for v in range(variables):
                at = [grid.tile_of(increment, v * levels + l, start // SUBLANES + j) for j in range(2)]
                weighted.append(factor * obs_weight[v] * jnp.concatenate([increment[at[0]], increment[at[1]]], axis=0))
            for m in range(members):
                total = perturb[m, 0, l, start : start + tile, :].astype(jnp.float32) * weighted[0]
                for v in range(1, variables):
                    total = total + perturb[m, v, l, start : start + tile, :].astype(jnp.float32) * weighted[v]
                base = (m * levels + l) * rows
                back[base + start : base + start + tile, :] = total
        slot, sub = divmod(l * STEPS, SUBLANES)
        slot += levels * 2 * STEPS + levels
        counts = ordered(odd, got_far[slot, sub : sub + STEPS, :], got_near[slot, sub : sub + STEPS, :])
        counts = [jnp.concatenate([c, c], axis=0) * (scale * scale) for c in counts]
        totals = [[0.0] * pairs, [0.0] * pairs]
        for v in range(variables):
            both = increment[grid.tile_of(increment, v * levels + l, rows // SUBLANES)]
            after = jnp.where(upper(), both, turned(both))
            before = jnp.where(upper(), turned(both), both)
            weighted = [c * obs_weight[v] * w for c, w in zip(counts, (after, before))]
            for q in range(pairs):
                at = (v * levels + l) * pairs + q
                for side, p in enumerate(ordered(odd, rim_far[at], rim_near[at])):
                    totals[side][q] = totals[side][q] + p * weighted[side]
        for q in range(pairs):
            at = slice((l * pairs + q) * SUBLANES, (l * pairs + q + 1) * SUBLANES)
            back_after[at, :] = totals[0][q]
            back_before[at, :] = totals[1][q]
    field_columns(grid, lambda l, k: grid.ring_row(back, back_before, back_after, l, k), grid.ring, near, far, edges)


def adjoint_kernel(grid, control, main, edges, strip_ring, col_near, col_far, out, strip_keep, ends):
    strip_steps(grid, adjoint_steps, edges, grid.ring, STEPS, col_near, col_far, strip_ring, strip_keep, ends)
    for l in range(grid.levels):
        for y in range(grid.rows):
            at = grid.members_at(l, y)
            out[at, :] = control[at, :] + merged(grid, main[l * grid.rows + y], ends[y], l)


def shape_of(*shape):
    return jax.ShapeDtypeStruct(shape, jnp.float32)


def shards(control, perturb, obs_count, obs_weight, diffusivity):
    members, levels, rows, lanes = control.shape
    variables = perturb.shape[1]
    ways = lax.axis_size("mem")
    scale = 1.0 / math.sqrt(members * ways - 1)
    count = members * levels
    grid = Grid(members, levels, rows)
    assert members == SUBLANES and lanes == LANES and grid.block >= 8 * STEPS
    vmem = pl.BlockSpec(memory_space=pltpu.VMEM)
    hbm = pl.BlockSpec(memory_space=pltpu.HBM)
    f32 = jnp.float32

    def call(kernel, *args, work=0, **kwargs):
        cost = pl.CostEstimate(flops=work, bytes_accessed=work, transcendentals=0) if work else None
        return pl.pallas_call(
            lambda *refs: kernel(grid, *refs), compiler_params=PARAMS, cost_estimate=cost, **kwargs
        )(*args)

    def in_hbm(array):
        return pltpu.with_memory_space_constraint(array, pltpu.HBM)

    depth = 2 * STEPS
    ring_shape, strip_shape = (levels * grid.wide, lanes), (grid.padded, lanes)
    rim = shape_of(count * STEPS, lanes)

    def tiles(number):
        return shape_of(number, SUBLANES, lanes)

    edge = tiles(levels * depth + levels + -(-levels * STEPS // SUBLANES))
    level_rows = shape_of(levels * rows, lanes)
    near, far, flat, flat_diff, seen = call(
        rows_kernel,
        in_hbm(control.reshape(count * rows, lanes)),
        in_hbm(diffusivity.reshape(levels * rows, lanes)),
        in_hbm(obs_count.reshape(levels * rows, lanes)),
        out_shape=(edge, edge, shape_of(count * rows, lanes), level_rows, level_rows),
        in_specs=[hbm] * 3,
        scratch_shapes=[pltpu.VMEM(level_rows.shape, jnp.int32), pltpu.SemaphoreType.DMA((3,))],
    )
    got = swap(near, far, "gy")
    edge = tiles(variables * levels * members // 2)
    near, far, held = call(
        perturb_rows_kernel,
        flat_diff,
        in_hbm(perturb),
        work=8 << 20,
        out_shape=(edge, edge, jax.ShapeDtypeStruct(perturb.shape, perturb.dtype)),
        in_specs=[vmem, hbm],
        scratch_shapes=[pltpu.SemaphoreType.DMA((members // 2,))],
    )
    rims = swap(near, far, "gy")
    edge = tiles(grid.wide_packs + 1)
    near, far, edges, ring, ring_edges = call(
        columns_kernel,
        flat,
        flat_diff,
        *got,
        out_shape=(edge, edge, tiles(grid.wide), shape_of(*ring_shape), shape_of(*strip_shape)),
    )
    sides = swap(near, far, "gx")
    main = call(
        spread_main_kernel,
        flat,
        ring,
        *got,
        work=6 << 20,
        out_shape=tiles(levels * grid.ring),
        scratch_shapes=[pltpu.VMEM(ring_shape, f32)],
    )
    piece = -(-variables * levels * grid.ring // (ways * SUBLANES)) * SUBLANES
    partial, strip_ring = call(
        spread_kernel,
        main,
        edges,
        ring_edges,
        *sides,
        held,
        *rims,
        out_shape=(shape_of(ways, piece, lanes), shape_of(*strip_shape)),
        scratch_shapes=[
            pltpu.VMEM(strip_shape, f32),
            pltpu.VMEM((grid.ring, SUBLANES, lanes), f32),
            pltpu.VMEM((count * rows, lanes), f32),
            pltpu.VMEM(rim.shape, f32),
            pltpu.VMEM(rim.shape, f32),
        ],
    )

    parts = lax.all_to_all(partial, "mem", 0, 0)
    mine = jnp.sum(parts, axis=0)
    increment = lax.all_to_all(jnp.broadcast_to(mine, parts.shape), "mem", 0, 0)

    edge = tiles(grid.packs)
    back, before, after, edges, near, far = call(
        lambda grid, *refs: back_kernel(grid, scale, *refs),
        increment,
        seen,
        obs_weight,
        held,
        *rims,
        *got,
        out_shape=(shape_of(count * rows, lanes), rim, rim, tiles(grid.ring), edge, edge),
        in_specs=[vmem, vmem, pl.BlockSpec(memory_space=pltpu.SMEM)] + [vmem] * 5,
    )
    sides = swap(near, far, "gx")
    main = call(
        adjoint_main_kernel,
        back,
        before,
        after,
        ring,
        work=6 << 20,
        out_shape=tiles(levels * rows),
        scratch_shapes=[pltpu.VMEM(ring_shape, f32)],
    )
    out = call(
        adjoint_kernel,
        flat,
        main,
        edges,
        strip_ring,
        *sides,
        out_shape=shape_of(count * rows, lanes),
        scratch_shapes=[pltpu.VMEM(strip_shape, f32), pltpu.VMEM((rows, SUBLANES, lanes), f32)],
    )
    return out.reshape(control.shape)


def solution(mesh):
    placed = (
        P("mem", None, "gy", "gx"),
        P("mem", None, None, "gy", "gx"),
        P(None, "gy", "gx"),
        P(),
        P(None, "gy", "gx"),
    )

    return jax.shard_map(shards, mesh=mesh, in_specs=placed, out_specs=P("mem", None, "gy", "gx"), check_vma=False)
```

```python
import math

import jax
import jax.numpy as jnp
from jax import lax
from jax.experimental import pallas as pl
from jax.experimental.pallas import tpu as pltpu
from jax.sharding import PartitionSpec as P


STEPS = 4
LANES = 128
SUBLANES = 8
PARAMS = pltpu.CompilerParams(vmem_limit_bytes=16 << 20)


def swap(near, far, axis):
    size = lax.axis_size(axis)
    out = []
    for value, start in ((near, 0), (far, 1)):
        pairs = []
        for i in range(start, size - 1, 2):
            pairs += [(i, i + 1), (i + 1, i)]
        out.append(lax.ppermute(value, axis, pairs))
    return out


def is_odd(axis):
    return lax.rem(lax.axis_index(axis), 2) == 1


def ordered(odd, first, last):
    return jnp.where(odd, first, last), jnp.where(odd, last, first)


class Grid:
    def __init__(self, members, levels, rows):
        self.members, self.levels, self.rows = members, levels, rows
        self.wide = rows + 4 * STEPS
        self.ring = rows + 2 * STEPS
        self.block = LANES // levels // STEPS * STEPS
        self.per = self.block // STEPS
        self.wide_packs = -(-self.wide // self.per)
        self.packs = -(-self.ring // self.per)
        self.padded = -(-self.wide_packs * self.per // SUBLANES) * SUBLANES

    def members_at(self, level, y):
        return pl.ds(level * self.rows + y, self.members, stride=self.levels * self.rows)

    def rim_at(self, level, r):
        return pl.ds(level * self.members * STEPS + r, self.members, stride=STEPS)

    def wide_row(self, field, got, odd, level, k):
        y = k - 2 * STEPS
        if 0 <= y < self.rows:
            return field[self.members_at(level, y), :]
        before = y < 0
        at = level * 2 * STEPS + (k if before else y - self.rows)
        near, far = got
        after_value, before_value = ordered(odd, far[at], near[at])
        return before_value if before else after_value

    def ring_row(self, field, before, after, level, k):
        y = k - STEPS
        if y < 0:
            return before[self.rim_at(level, k), :]
        if y >= self.rows:
            return after[self.rim_at(level, y - self.rows), :]
        return field[self.members_at(level, y), :]

    def tile_of(self, ref, plane, j):
        t = plane * (self.ring // SUBLANES) + j
        return t // (ref.shape[1] // SUBLANES), pl.ds(t % (ref.shape[1] // SUBLANES) * SUBLANES, SUBLANES)

    def lanes(self, rows=SUBLANES):
        lane = lax.broadcasted_iota(jnp.int32, (rows, LANES), 1)
        return lax.rem(lane, self.block)


def within(place, start, size):
    return (place >= start) & (place < start + size)


def rolled(value, shift):
    shift %= LANES
    return pltpu.roll(value, shift, 1) if shift else value


def edges_of(grid, value_of, rows=SUBLANES):
    lane = lax.broadcasted_iota(jnp.int32, (rows, LANES), 1)
    out = jnp.zeros((rows, LANES), jnp.float32)
    for l in range(grid.levels):
        base = l * grid.block
        out = jnp.where(within(lane, base, 4 * STEPS), rolled(value_of(l), base + 2 * STEPS), out)
    return out


def packed(grid, edges, rows=SUBLANES):
    place = grid.lanes(rows)
    first = jnp.zeros((rows, LANES), jnp.float32)
    last = first
    for i, value in enumerate(edges):
        mask = within(place, i * STEPS, STEPS)
        first = jnp.where(mask, rolled(value, (i - 2) * STEPS), first)
        last = jnp.where(mask, rolled(value, (i - 1) * STEPS), last)
    return first, last


def strip_of(grid, edges, west, east, i, rows=SUBLANES):
    place = grid.lanes(rows)
    out = jnp.where(place < 2 * STEPS, edges, 0.0)
    out = jnp.where(within(place, 6 * STEPS, 2 * STEPS), rolled(edges, 4 * STEPS), out)
    out = jnp.where(within(place, 2 * STEPS, STEPS), rolled(east, (2 - i) * STEPS), out)
    return jnp.where(within(place, 5 * STEPS, STEPS), rolled(west, (5 - i) * STEPS), out)


def joined(grid, strip):
    return jnp.where(grid.lanes() < 2 * STEPS, strip, rolled(strip, -4 * STEPS))


def merged(grid, main, ends, level):
    lane = lax.broadcasted_iota(jnp.int32, (SUBLANES, LANES), 1)
    outer = (lane < STEPS) | (lane >= LANES - STEPS)
    return jnp.where(outer, rolled(ends, LANES - 2 * STEPS - level * grid.block), main)


def lateral(value):
    return pltpu.roll(value, 1, 1) + pltpu.roll(value, LANES - 1, 1)


def spread_steps(field, coef, keep):
    for s in range(1, STEPS + 1):
        new = list(field)
        for k in range(s, len(field) - s):
            around = (field[k - 1] + field[k + 1]) + lateral(field[k])
            new[k] = keep(k) * field[k] + coef(k) * around
        field = new
    return field[STEPS:-STEPS]


def adjoint_steps(field, coef, keep):
    for s in range(1, STEPS + 1):
        flux = {k: coef(k) * field[k] for k in range(s - 1, len(field) - s + 1)}
        new = list(field)
        for k in range(s, len(field) - s):
            new[k] = keep(k) * field[k] + ((flux[k - 1] + flux[k + 1]) + lateral(flux[k]))
        field = new
    return field[STEPS:-STEPS]


def row_reader(ref, start):
    return lambda k: jnp.broadcast_to(ref[pl.ds(start + k, 1), :], (SUBLANES, LANES))


def rows_kernel(
    grid, control_hbm, diffusivity_hbm, count_hbm, weight_hbm, near, far, control, diffusivity, seen, weights, count, weight, sems
):
    levels, rows = grid.levels, grid.rows
    depth = 2 * STEPS
    copies = [
        pltpu.make_async_copy(diffusivity_hbm, diffusivity, sems.at[0]),
        pltpu.make_async_copy(count_hbm, count, sems.at[1]),
        pltpu.make_async_copy(control_hbm, control, sems.at[2]),
        pltpu.make_async_copy(weight_hbm, weight, sems.at[3]),
    ]
    for copy in copies:
        copy.start()
    odd = is_odd("gy")
    copies[3].wait()
    for v in range(weights.shape[0]):
        weights[v] = jnp.full((SUBLANES, LANES), weight[v])
    copies[0].wait()
    copies[1].wait()
    seen[...] = count[...].astype(jnp.float32)
    at = levels * depth
    for l in range(levels):
        first = diffusivity[l * rows : l * rows + depth, :]
        last = diffusivity[(l + 1) * rows - depth : (l + 1) * rows, :]
        near[at + l], far[at + l] = ordered(odd, first, last)
        first = seen[l * rows : l * rows + STEPS, :]
        last = seen[(l + 1) * rows - STEPS : (l + 1) * rows, :]
        slot, sub = divmod(l * STEPS, SUBLANES)
        a, b = ordered(odd, first, last)
        near[at + levels + slot, sub : sub + STEPS, :] = a
        far[at + levels + slot, sub : sub + STEPS, :] = b
    copies[2].wait()
    for l in range(levels):
        for r in range(depth):
            first = control[grid.members_at(l, r), :]
            last = control[grid.members_at(l, rows - depth + r), :]
            near[l * depth + r], far[l * depth + r] = ordered(odd, first, last)


def turned(value):
    return pltpu.roll(value, STEPS, 0)


def upper():
    return lax.broadcasted_iota(jnp.int32, (SUBLANES, LANES), 0) < STEPS


def perturb_rows_kernel(grid, order, perturb_hbm, near, far, heads, tails, sems):
    members, variables, levels, rows, _ = perturb_hbm.shape
    copies = [
        pltpu.make_async_copy(perturb_hbm.at[:, :, :, pl.ds(0, SUBLANES), :], heads, sems.at[0]),
        pltpu.make_async_copy(perturb_hbm.at[:, :, :, pl.ds(rows - SUBLANES, SUBLANES), :], tails, sems.at[1]),
    ]
    for copy in copies:
        copy.start()
    for copy in copies:
        copy.wait()
    odd = is_odd("gy")
    for q in range(members // 2):
        for v in range(variables):
            for l in range(levels):
                head = [heads[2 * q + j, v, l].astype(jnp.float32) for j in range(2)]
                tail = [tails[2 * q + j, v, l].astype(jnp.float32) for j in range(2)]
                first = jnp.where(upper(), head[0], turned(head[1]))
                last = jnp.where(upper(), turned(tail[0]), tail[1])
                at = (v * levels + l) * (members // 2) + q
                near[at], far[at] = ordered(odd, first, last)


def field_columns(grid, row_of, length, near, far, edges):
    for start in range(0, length, grid.per):
        here = []
        for k in range(start, min(length, start + grid.per)):
            here.append(edges_of(grid, lambda l: row_of(l, k)))
            edges[k] = here[-1]
        q = start // grid.per
        near[q], far[q] = ordered(is_odd("gx"), *packed(grid, here))


def columns_kernel(grid, control, diffusivity, got_near, got_far, near, far, edges, ring, ring_edges):
    got = (got_near, got_far)
    odd = is_odd("gy")
    field_columns(grid, lambda l, k: grid.wide_row(control, got, odd, l, k), grid.wide, near, far, edges)
    depth = 2 * STEPS
    for l in range(grid.levels):
        after, before = ordered(odd, got_far[grid.levels * depth + l], got_near[grid.levels * depth + l])
        base = l * grid.wide
        ring[base : base + depth, :] = before
        ring[base + depth : base + depth + grid.rows, :] = diffusivity[l * grid.rows : (l + 1) * grid.rows, :]
        ring[base + depth + grid.rows : base + grid.wide, :] = after
    ring_edges[...] = jnp.zeros(ring_edges.shape, jnp.float32)
    ring_edges[: grid.wide, :] = edges_of(grid, lambda l: ring[l * grid.wide : (l + 1) * grid.wide, :], grid.wide)
    packs = grid.wide_packs
    spaced = [ring_edges[pl.ds(i, packs, stride=grid.per), :] for i in range(grid.per)]
    a, b = ordered(is_odd("gx"), *packed(grid, spaced, packs))
    near[packs, :packs, :] = a
    far[packs, :packs, :] = b


def spread_main_kernel(grid, control, ring, got_near, got_far, perturb_hbm, main, perturb, keep, sem):
    copy = pltpu.make_async_copy(perturb_hbm, perturb, sem)
    copy.start()
    odd = is_odd("gy")
    keep[...] = 1.0 - 4.0 * ring[...]
    for l in range(grid.levels):
        rows = [grid.wide_row(control, (got_near, got_far), odd, l, k) for k in range(grid.wide)]
        at = l * grid.wide
        for y, row in enumerate(spread_steps(rows, row_reader(ring, at), row_reader(keep, at))):
            main[l * grid.ring + y] = row
    copy.wait()


def adjoint_main_kernel(grid, back, before, after, ring, main, keep):
    keep[...] = 1.0 - 4.0 * ring[...]
    for l in range(grid.levels):
        rows = [grid.ring_row(back, before, after, l, k) for k in range(grid.ring)]
        at = l * grid.wide + STEPS
        for y, row in enumerate(adjoint_steps(rows, row_reader(ring, at), row_reader(keep, at))):
            main[l * grid.rows + y] = row


def sides(col_near, col_far, q):
    east, west = ordered(is_odd("gx"), col_far[q], col_near[q])
    return west, east


def strip_steps(grid, steps, edges, length, skip, col_near, col_far, strip_ring, strip_keep, ends):
    strip_keep[...] = 1.0 - 4.0 * strip_ring[...]
    field = []
    for k in range(length):
        q, i = divmod(k, grid.per)
        field.append(strip_of(grid, edges[k], *sides(col_near, col_far, q), i))
    for y, strip in enumerate(steps(field, row_reader(strip_ring, skip), row_reader(strip_keep, skip))):
        ends[y] = joined(grid, strip)


def spread_kernel(
    grid,
    main,
    edges,
    ring_edges,
    col_near,
    col_far,
    perturb,
    rim_near,
    rim_far,
    partial,
    strip_ring,
    strip_keep,
    ends,
    spread,
    spread_before,
    spread_after,
):
    packs = grid.wide_packs
    west, east = (side[:packs] for side in sides(col_near, col_far, packs))
    strip_ring[...] = jnp.zeros(strip_ring.shape, jnp.float32)
    for i in range(grid.per):
        at = pl.ds(i, packs, stride=grid.per)
        strip_ring[at, :] = strip_of(grid, ring_edges[at, :], west, east, i, packs)
    strip_steps(grid, spread_steps, edges, grid.wide, 0, col_near, col_far, strip_ring, strip_keep, ends)
    members, variables, levels, rows, _ = perturb.shape
    for l in range(levels):
        for j in range(grid.ring):
            value = merged(grid, main[l * grid.ring + j], ends[j], l)
            y = j - STEPS
            if y < 0:
                spread_before[grid.rim_at(l, j), :] = value
            elif y >= rows:
                spread_after[grid.rim_at(l, y - rows), :] = value
            else:
                spread[grid.members_at(l, y), :] = value
    tile = 2 * SUBLANES
    odd = is_odd("gy")
    pairs = members // 2
    for l in range(levels):
        for start in range(0, rows, tile):
            here = [spread[(m * levels + l) * rows + start : (m * levels + l) * rows + start + tile, :] for m in range(members)]
            for v in range(variables):
                total = perturb[0, v, l, start : start + tile, :].astype(jnp.float32) * here[0]
                for m in range(1, members):
                    total = total + perturb[m, v, l, start : start + tile, :].astype(jnp.float32) * here[m]
                for j in range(2):
                    partial[grid.tile_of(partial, v * levels + l, start // SUBLANES + j)] = total[j * SUBLANES : (j + 1) * SUBLANES]
        rims = [(after, before) for after, before in zip(
            [spread_after[(l * pairs + q) * SUBLANES : (l * pairs + q + 1) * SUBLANES, :] for q in range(pairs)],
            [spread_before[(l * pairs + q) * SUBLANES : (l * pairs + q + 1) * SUBLANES, :] for q in range(pairs)],
        )]
        for v in range(variables):
            totals = [0.0, 0.0]
            for q in range(pairs):
                at = (v * levels + l) * pairs + q
                outer = ordered(odd, rim_far[at], rim_near[at])
                totals = [t + p * r for t, p, r in zip(totals, outer, rims[q])]
            after, before = (t + turned(t) for t in totals)
            partial[grid.tile_of(partial, v * levels + l, rows // SUBLANES)] = jnp.where(upper(), after, before)
    used = variables * levels * (grid.ring // SUBLANES)
    for t in range(used, partial.shape[0] * partial.shape[1] // SUBLANES):
        partial[grid.tile_of(partial, 0, t)] = jnp.zeros((SUBLANES, LANES), jnp.float32)


def back_kernel(
    grid,
    scale,
    increment,
    seen,
    weights,
    perturb,
    rim_near,
    rim_far,
    got_near,
    got_far,
    back,
    back_before,
    back_after,
    edges,
    near,
    far,
):
    members, variables, levels, rows, _ = perturb.shape
    tile = 2 * SUBLANES
    odd = is_odd("gy")
    pairs = members // 2
    for l in range(levels):
        for start in range(0, rows, tile):
            factor = seen[l * rows + start : l * rows + start + tile, :] * (scale * scale)
            weighted = []
            for v in range(variables):
                at = [grid.tile_of(increment, v * levels + l, start // SUBLANES + j) for j in range(2)]
                pair = [weights[v] * increment[a] for a in at]
                weighted.append(factor * jnp.concatenate(pair, axis=0))
            for m in range(members):
                total = perturb[m, 0, l, start : start + tile, :].astype(jnp.float32) * weighted[0]
                for v in range(1, variables):
                    total = total + perturb[m, v, l, start : start + tile, :].astype(jnp.float32) * weighted[v]
                base = (m * levels + l) * rows
                back[base + start : base + start + tile, :] = total
        slot, sub = divmod(l * STEPS, SUBLANES)
        slot += levels * 2 * STEPS + levels
        counts = ordered(odd, got_far[slot, sub : sub + STEPS, :], got_near[slot, sub : sub + STEPS, :])
        counts = [jnp.concatenate([c, c], axis=0) * (scale * scale) for c in counts]
        totals = [[0.0] * pairs, [0.0] * pairs]
        for v in range(variables):
            both = increment[grid.tile_of(increment, v * levels + l, rows // SUBLANES)]
            after = jnp.where(upper(), both, turned(both))
            before = jnp.where(upper(), turned(both), both)
            weighted = [c * (weights[v] * w) for c, w in zip(counts, (after, before))]
            for q in range(pairs):
                at = (v * levels + l) * pairs + q
                for side, p in enumerate(ordered(odd, rim_far[at], rim_near[at])):
                    totals[side][q] = totals[side][q] + p * weighted[side]
        for q in range(pairs):
            at = slice((l * pairs + q) * SUBLANES, (l * pairs + q + 1) * SUBLANES)
            back_after[at, :] = totals[0][q]
            back_before[at, :] = totals[1][q]
    field_columns(grid, lambda l, k: grid.ring_row(back, back_before, back_after, l, k), grid.ring, near, far, edges)


def adjoint_kernel(grid, control, main, edges, strip_ring, col_near, col_far, out_hbm, strip_keep, ends, out, sems):
    strip_steps(grid, adjoint_steps, edges, grid.ring, STEPS, col_near, col_far, strip_ring, strip_keep, ends)
    planes = (grid.members * grid.levels, grid.rows, LANES)
    copies = []
    for start in range(0, grid.rows, SUBLANES):
        for l in range(grid.levels):
            for y in range(start, start + SUBLANES):
                at = grid.members_at(l, y)
                out[at, :] = control[at, :] + merged(grid, main[l * grid.rows + y], ends[y], l)
        part = pl.ds(start, SUBLANES)
        copies.append(pltpu.make_async_copy(out.reshape(planes).at[:, part, :], out_hbm.at[:, part, :], sems.at[start // SUBLANES]))
        copies[-1].start()
    for copy in copies:
        copy.wait()


def shape_of(*shape):
    return jax.ShapeDtypeStruct(shape, jnp.float32)


def shards(control, perturb, obs_count, obs_weight, diffusivity):
    members, levels, rows, lanes = control.shape
    variables = perturb.shape[1]
    ways = lax.axis_size("mem")
    scale = 1.0 / math.sqrt(members * ways - 1)
    count = members * levels
    grid = Grid(members, levels, rows)
    assert members == SUBLANES and lanes == LANES and grid.block >= 8 * STEPS
    vmem = pl.BlockSpec(memory_space=pltpu.VMEM)
    hbm = pl.BlockSpec(memory_space=pltpu.HBM)
    f32 = jnp.float32

    def call(kernel, *args, work=0, **kwargs):
        cost = pl.CostEstimate(flops=work, bytes_accessed=work, transcendentals=0) if work else None
        return pl.pallas_call(
            lambda *refs: kernel(grid, *refs), compiler_params=PARAMS, cost_estimate=cost, **kwargs
        )(*args)

    def in_hbm(array):
        return pltpu.with_memory_space_constraint(array, pltpu.HBM)

    depth = 2 * STEPS
    ring_shape, strip_shape = (levels * grid.wide, lanes), (grid.padded, lanes)
    rim = shape_of(count * STEPS, lanes)

    def tiles(number):
        return shape_of(number, SUBLANES, lanes)

    edge = tiles(levels * depth + levels + -(-levels * STEPS // SUBLANES))
    level_rows = shape_of(levels * rows, lanes)
    near, far, flat, flat_diff, seen, weights = call(
        rows_kernel,
        in_hbm(control.reshape(count * rows, lanes)),
        in_hbm(diffusivity.reshape(levels * rows, lanes)),
        in_hbm(obs_count.reshape(levels * rows, lanes)),
        in_hbm(obs_weight),
        out_shape=(edge, edge, shape_of(count * rows, lanes), level_rows, level_rows, tiles(variables)),
        in_specs=[hbm] * 4,
        scratch_shapes=[
            pltpu.VMEM(level_rows.shape, jnp.int32),
            pltpu.SMEM(obs_weight.shape, f32),
            pltpu.SemaphoreType.DMA((4,)),
        ],
    )
    got = swap(near, far, "gy")
    edge = tiles(variables * levels * members // 2)
    edge_rows = pltpu.VMEM((members, variables, levels, SUBLANES, lanes), perturb.dtype)
    near, far = call(
        perturb_rows_kernel,
        flat_diff,
        in_hbm(perturb),
        work=8 << 20,
        out_shape=(edge, edge),
        in_specs=[vmem, hbm],
        scratch_shapes=[edge_rows, edge_rows, pltpu.SemaphoreType.DMA((2,))],
    )
    rims = swap(near, far, "gy")
    edge = tiles(grid.wide_packs + 1)
    near, far, edges, ring, ring_edges = call(
        columns_kernel,
        flat,
        flat_diff,
        *got,
        out_shape=(edge, edge, tiles(grid.wide), shape_of(*ring_shape), shape_of(*strip_shape)),
    )
    sides = swap(near, far, "gx")
    main, held = call(
        spread_main_kernel,
        flat,
        ring,
        *got,
        in_hbm(perturb),
        work=6 << 20,
        out_shape=(tiles(levels * grid.ring), jax.ShapeDtypeStruct(perturb.shape, perturb.dtype)),
        in_specs=[vmem] * 4 + [hbm],
        scratch_shapes=[pltpu.VMEM(ring_shape, f32), pltpu.SemaphoreType.DMA],
    )
    piece = -(-variables * levels * grid.ring // (ways * SUBLANES)) * SUBLANES
    partial, strip_ring = call(
        spread_kernel,
        main,
        edges,
        ring_edges,
        *sides,
        held,
        *rims,
        out_shape=(shape_of(ways, piece, lanes), shape_of(*strip_shape)),
        scratch_shapes=[
            pltpu.VMEM(strip_shape, f32),
            pltpu.VMEM((grid.ring, SUBLANES, lanes), f32),
            pltpu.VMEM((count * rows, lanes), f32),
            pltpu.VMEM(rim.shape, f32),
            pltpu.VMEM(rim.shape, f32),
        ],
    )

    parts = lax.all_to_all(partial, "mem", 0, 0)
    mine = jnp.sum(parts, axis=0)
    increment = lax.all_to_all(jnp.broadcast_to(mine, parts.shape), "mem", 0, 0)

    edge = tiles(grid.packs)
    back, before, after, edges, near, far = call(
        lambda grid, *refs: back_kernel(grid, scale, *refs),
        increment,
        seen,
        weights,
        held,
        *rims,
        *got,
        out_shape=(shape_of(count * rows, lanes), rim, rim, tiles(grid.ring), edge, edge),
    )
    sides = swap(near, far, "gx")
    main = call(
        adjoint_main_kernel,
        back,
        before,
        after,
        ring,
        work=6 << 20,
        out_shape=tiles(levels * rows),
        scratch_shapes=[pltpu.VMEM(ring_shape, f32)],
    )
    out = call(
        adjoint_kernel,
        flat,
        main,
        edges,
        strip_ring,
        *sides,
        out_shape=shape_of(count, rows, lanes),
        out_specs=hbm,
        scratch_shapes=[
            pltpu.VMEM(strip_shape, f32),
            pltpu.VMEM((rows, SUBLANES, lanes), f32),
            pltpu.VMEM((count * rows, lanes), f32),
            pltpu.SemaphoreType.DMA((rows // SUBLANES,)),
        ],
    )
    return out.reshape(control.shape)


def solution(mesh):
    placed = (
        P("mem", None, "gy", "gx"),
        P("mem", None, None, "gy", "gx"),
        P(None, "gy", "gx"),
        P(),
        P(None, "gy", "gx"),
    )

    return jax.shard_map(shards, mesh=mesh, in_specs=placed, out_specs=P("mem", None, "gy", "gx"), check_vma=False)
```

```python
import math

import jax
import jax.numpy as jnp
from jax import lax
from jax.experimental import pallas as pl
from jax.experimental.pallas import tpu as pltpu
from jax.sharding import PartitionSpec as P


STEPS = 4
LANES = 128
SUBLANES = 8
PARAMS = pltpu.CompilerParams(vmem_limit_bytes=16 << 20)


def swap(near, far, axis):
    size = lax.axis_size(axis)
    out = []
    for value, start in ((near, 0), (far, 1)):
        pairs = []
        for i in range(start, size - 1, 2):
            pairs += [(i, i + 1), (i + 1, i)]
        out.append(lax.ppermute(value, axis, pairs))
    return out


def is_odd(axis):
    return lax.rem(lax.axis_index(axis), 2) == 1


def ordered(odd, first, last):
    return jnp.where(odd, first, last), jnp.where(odd, last, first)


class Grid:
    def __init__(self, members, levels, rows):
        self.members, self.levels, self.rows = members, levels, rows
        self.wide = rows + 4 * STEPS
        self.ring = rows + 2 * STEPS
        self.block = LANES // levels // STEPS * STEPS
        self.per = self.block // STEPS
        self.wide_packs = -(-self.wide // self.per)
        self.packs = -(-self.ring // self.per)
        self.padded = self.per * SUBLANES

    def members_at(self, level, y):
        return pl.ds(level * self.rows + y, self.members, stride=self.levels * self.rows)

    def rim_at(self, level, r):
        return pl.ds(level * self.members * STEPS + r, self.members, stride=STEPS)

    def wide_row(self, field, got, odd, level, k):
        y = k - 2 * STEPS
        if 0 <= y < self.rows:
            return field[self.members_at(level, y), :]
        before = y < 0
        at = level * 2 * STEPS + (k if before else y - self.rows)
        near, far = got
        after_value, before_value = ordered(odd, far[at], near[at])
        return before_value if before else after_value

    def ring_row(self, field, before, after, level, k):
        y = k - STEPS
        if y < 0:
            return before[self.rim_at(level, k), :]
        if y >= self.rows:
            return after[self.rim_at(level, y - self.rows), :]
        return field[self.members_at(level, y), :]

    def set_ring_row(self, field, before, after, level, k, value):
        y = k - STEPS
        if y < 0:
            before[self.rim_at(level, k), :] = value
        elif y >= self.rows:
            after[self.rim_at(level, y - self.rows), :] = value
        else:
            field[self.members_at(level, y), :] = value

    def tile_of(self, ref, plane, j):
        t = plane * (self.ring // SUBLANES) + j
        return t // (ref.shape[1] // SUBLANES), pl.ds(t % (ref.shape[1] // SUBLANES) * SUBLANES, SUBLANES)

    def lanes(self, rows=SUBLANES):
        lane = lax.broadcasted_iota(jnp.int32, (rows, LANES), 1)
        return lax.rem(lane, self.block)


def within(place, start, size):
    return (place >= start) & (place < start + size)


def rolled(value, shift):
    shift %= LANES
    return pltpu.roll(value, shift, 1) if shift else value


def edges_of(grid, value_of, rows=SUBLANES):
    lane = lax.broadcasted_iota(jnp.int32, (rows, LANES), 1)
    out = jnp.zeros((rows, LANES), jnp.float32)
    for l in range(grid.levels):
        base = l * grid.block
        out = jnp.where(within(lane, base, 4 * STEPS), rolled(value_of(l), base + 2 * STEPS), out)
    return out


def packed(grid, edges, rows=SUBLANES):
    place = grid.lanes(rows)
    first = jnp.zeros((rows, LANES), jnp.float32)
    last = first
    for i, value in enumerate(edges):
        mask = within(place, i * STEPS, STEPS)
        first = jnp.where(mask, rolled(value, (i - 2) * STEPS), first)
        last = jnp.where(mask, rolled(value, (i - 1) * STEPS), last)
    return first, last


def strip_of(grid, edges, west, east, i, rows=SUBLANES):
    place = grid.lanes(rows)
    out = jnp.where(place < 2 * STEPS, edges, 0.0)
    out = jnp.where(within(place, 6 * STEPS, 2 * STEPS), rolled(edges, 4 * STEPS), out)
    out = jnp.where(within(place, 2 * STEPS, STEPS), rolled(east, (2 - i) * STEPS), out)
    return jnp.where(within(place, 5 * STEPS, STEPS), rolled(west, (5 - i) * STEPS), out)


def joined(grid, strip):
    return jnp.where(grid.lanes() < 2 * STEPS, strip, rolled(strip, -4 * STEPS))


def merged(grid, main, ends, level):
    lane = lax.broadcasted_iota(jnp.int32, main.shape, 1)
    outer = (lane < STEPS) | (lane >= LANES - STEPS)
    return jnp.where(outer, rolled(ends, LANES - 2 * STEPS - level * grid.block), main)


def lateral(value):
    return pltpu.roll(value, 1, 1) + pltpu.roll(value, LANES - 1, 1)


def spread_steps(field, coef, keep):
    for s in range(1, STEPS + 1):
        new = list(field)
        for k in range(s, len(field) - s):
            around = (field[k - 1] + field[k + 1]) + lateral(field[k])
            new[k] = keep(k) * field[k] + coef(k) * around
        field = new
    return field[STEPS:-STEPS]


def adjoint_steps(field, coef, keep):
    for s in range(1, STEPS + 1):
        flux = {k: coef(k) * field[k] for k in range(s - 1, len(field) - s + 1)}
        new = list(field)
        for k in range(s, len(field) - s):
            new[k] = keep(k) * field[k] + ((flux[k - 1] + flux[k + 1]) + lateral(flux[k]))
        field = new
    return field[STEPS:-STEPS]


def row_reader(ref, start):
    return lambda k: jnp.broadcast_to(ref[pl.ds(start + k, 1), :], (SUBLANES, LANES))


def turned(value):
    return pltpu.roll(value, STEPS, 0)


def upper():
    return lax.broadcasted_iota(jnp.int32, (SUBLANES, LANES), 0) < STEPS


def rows_kernel(
    grid,
    control_hbm,
    diffusivity_hbm,
    count_hbm,
    weight_hbm,
    perturb_hbm,
    near,
    far,
    outer_near,
    outer_far,
    control,
    diffusivity,
    seen,
    weights,
    count,
    weight,
    heads,
    tails,
    sems,
):
    levels, rows = grid.levels, grid.rows
    depth = 2 * STEPS
    pairs = (
        (diffusivity_hbm, diffusivity),
        (count_hbm, count),
        (weight_hbm, weight),
        (control_hbm, control),
        (perturb_hbm.at[:, :, :, pl.ds(0, SUBLANES), :], heads),
        (perturb_hbm.at[:, :, :, pl.ds(rows - SUBLANES, SUBLANES), :], tails),
    )
    copies = [pltpu.make_async_copy(source, target, sems.at[i]) for i, (source, target) in enumerate(pairs)]
    for copy in copies:
        copy.start()
    odd = is_odd("gy")
    for copy in copies[:3]:
        copy.wait()
    for v in range(weights.shape[0]):
        weights[v] = jnp.full((SUBLANES, LANES), weight[v])
    seen[...] = count[...].astype(jnp.float32)
    at = levels * depth
    for l in range(levels):
        first = diffusivity[l * rows : l * rows + depth, :]
        last = diffusivity[(l + 1) * rows - depth : (l + 1) * rows, :]
        near[at + l], far[at + l] = ordered(odd, first, last)
        first = seen[l * rows : l * rows + STEPS, :]
        last = seen[(l + 1) * rows - STEPS : (l + 1) * rows, :]
        slot, sub = divmod(l * STEPS, SUBLANES)
        a, b = ordered(odd, first, last)
        near[at + levels + slot, sub : sub + STEPS, :] = a
        far[at + levels + slot, sub : sub + STEPS, :] = b
    copies[3].wait()
    for l in range(levels):
        for r in range(depth):
            first = control[grid.members_at(l, r), :]
            last = control[grid.members_at(l, rows - depth + r), :]
            near[l * depth + r], far[l * depth + r] = ordered(odd, first, last)
    copies[4].wait()
    copies[5].wait()
    members, variables = heads.shape[:2]
    for q in range(members // 2):
        for v in range(variables):
            for l in range(levels):
                head = [heads[2 * q + j, v, l].astype(jnp.float32) for j in range(2)]
                tail = [tails[2 * q + j, v, l].astype(jnp.float32) for j in range(2)]
                first = jnp.where(upper(), head[0], turned(head[1]))
                last = jnp.where(upper(), turned(tail[0]), tail[1])
                at = (v * levels + l) * (members // 2) + q
                outer_near[at], outer_far[at] = ordered(odd, first, last)


def field_columns(grid, row_of, length, near, far, edges):
    for start in range(0, length, grid.per):
        here = []
        for k in range(start, min(length, start + grid.per)):
            here.append(edges_of(grid, lambda l: row_of(l, k)))
            edges[k] = here[-1]
        q = start // grid.per
        near[q], far[q] = ordered(is_odd("gx"), *packed(grid, here))


def columns_kernel(grid, control, diffusivity, got_near, got_far, near, far, edges, ring, ring_edges):
    got = (got_near, got_far)
    odd = is_odd("gy")
    field_columns(grid, lambda l, k: grid.wide_row(control, got, odd, l, k), grid.wide, near, far, edges)
    depth = 2 * STEPS
    for l in range(grid.levels):
        after, before = ordered(odd, got_far[grid.levels * depth + l], got_near[grid.levels * depth + l])
        base = l * grid.wide
        ring[base : base + depth, :] = before
        ring[base + depth : base + depth + grid.rows, :] = diffusivity[l * grid.rows : (l + 1) * grid.rows, :]
        ring[base + depth + grid.rows : base + grid.wide, :] = after
    ring_edges[...] = jnp.zeros(ring_edges.shape, jnp.float32)
    ring_edges[: grid.wide, :] = edges_of(grid, lambda l: ring[l * grid.wide : (l + 1) * grid.wide, :], grid.wide)
    packs = grid.wide_packs
    spaced = [ring_edges[pl.ds(i, packs, stride=grid.per), :] for i in range(grid.per)]
    a, b = ordered(is_odd("gx"), *packed(grid, spaced, packs))
    near[packs, :packs, :] = a
    far[packs, :packs, :] = b


def spread_main_kernel(grid, control, ring, got_near, got_far, perturb_hbm, main, main_before, main_after, perturb, keep, sem):
    copy = pltpu.make_async_copy(perturb_hbm, perturb, sem)
    copy.start()
    odd = is_odd("gy")
    keep[...] = 1.0 - 4.0 * ring[...]
    for l in range(grid.levels):
        rows = [grid.wide_row(control, (got_near, got_far), odd, l, k) for k in range(grid.wide)]
        at = l * grid.wide
        for k, row in enumerate(spread_steps(rows, row_reader(ring, at), row_reader(keep, at))):
            grid.set_ring_row(main, main_before, main_after, l, k, row)
    copy.wait()


def adjoint_main_kernel(grid, back, before, after, ring, main, keep):
    keep[...] = 1.0 - 4.0 * ring[...]
    for l in range(grid.levels):
        rows = [grid.ring_row(back, before, after, l, k) for k in range(grid.ring)]
        at = l * grid.wide + STEPS
        for y, row in enumerate(adjoint_steps(rows, row_reader(ring, at), row_reader(keep, at))):
            main[grid.members_at(l, y), :] = row


def sides(col_near, col_far, q):
    east, west = ordered(is_odd("gx"), col_far[q], col_near[q])
    return west, east


def strip_steps(grid, steps, edges, length, skip, col_near, col_far, strip_ring, strip_keep):
    strip_keep[...] = 1.0 - 4.0 * strip_ring[...]
    field = []
    for k in range(length):
        q, i = divmod(k, grid.per)
        field.append(strip_of(grid, edges[k], *sides(col_near, col_far, q), i))
    return [joined(grid, strip) for strip in steps(field, row_reader(strip_ring, skip), row_reader(strip_keep, skip))]


def spread_kernel(
    grid,
    main,
    main_before,
    main_after,
    edges,
    ring_edges,
    col_near,
    col_far,
    perturb,
    rim_near,
    rim_far,
    partial,
    strip_ring,
    strip_keep,
    ends,
    ends_before,
    ends_after,
):
    packs = grid.wide_packs
    west, east = (side[:packs] for side in sides(col_near, col_far, packs))
    strip_ring[...] = jnp.zeros(strip_ring.shape, jnp.float32)
    for i in range(grid.per):
        at = pl.ds(i, packs, stride=grid.per)
        strip_ring[at, :] = strip_of(grid, ring_edges[at, :], west, east, i, packs)
    members, variables, levels, rows, _ = perturb.shape
    one = Grid(members, 1, rows)
    for k, value in enumerate(strip_steps(grid, spread_steps, edges, grid.wide, 0, col_near, col_far, strip_ring, strip_keep)):
        one.set_ring_row(ends, ends_before, ends_after, 0, k, value)
    tile = 2 * SUBLANES
    odd = is_odd("gy")
    pairs = members // 2
    for l in range(levels):
        for start in range(0, rows, tile):
            here = []
            for m in range(members):
                at = pl.ds((m * levels + l) * rows + start, tile)
                here.append(merged(grid, main[at, :], ends[pl.ds(m * rows + start, tile), :], l))
            for v in range(variables):
                total = perturb[0, v, l, start : start + tile, :].astype(jnp.float32) * here[0]
                for m in range(1, members):
                    total = total + perturb[m, v, l, start : start + tile, :].astype(jnp.float32) * here[m]
                for j in range(2):
                    partial[grid.tile_of(partial, v * levels + l, start // SUBLANES + j)] = total[j * SUBLANES : (j + 1) * SUBLANES]
        rims = []
        for q in range(pairs):
            at, end_at = pl.ds((l * pairs + q) * SUBLANES, SUBLANES), pl.ds(q * SUBLANES, SUBLANES)
            both = ((main_after, ends_after), (main_before, ends_before))
            rims.append([merged(grid, m[at, :], e[end_at, :], l) for m, e in both])
        for v in range(variables):
            totals = [0.0, 0.0]
            for q in range(pairs):
                at = (v * levels + l) * pairs + q
                outer = ordered(odd, rim_far[at], rim_near[at])
                totals = [t + p * r for t, p, r in zip(totals, outer, rims[q])]
            after, before = (t + turned(t) for t in totals)
            partial[grid.tile_of(partial, v * levels + l, rows // SUBLANES)] = jnp.where(upper(), after, before)
    used = variables * levels * (grid.ring // SUBLANES)
    for t in range(used, partial.shape[0] * partial.shape[1] // SUBLANES):
        partial[grid.tile_of(partial, 0, t)] = jnp.zeros((SUBLANES, LANES), jnp.float32)


def back_kernel(
    grid,
    scale,
    increment,
    seen,
    weights,
    perturb,
    rim_near,
    rim_far,
    got_near,
    got_far,
    back,
    back_before,
    back_after,
    edges,
    near,
    far,
):
    members, variables, levels, rows, _ = perturb.shape
    tile = 2 * SUBLANES
    odd = is_odd("gy")
    pairs = members // 2
    for l in range(levels):
        for start in range(0, rows, tile):
            factor = seen[l * rows + start : l * rows + start + tile, :] * (scale * scale)
            weighted = []
            for v in range(variables):
                at = [grid.tile_of(increment, v * levels + l, start // SUBLANES + j) for j in range(2)]
                pair = [weights[v] * increment[a] for a in at]
                weighted.append(factor * jnp.concatenate(pair, axis=0))
            for m in range(members):
                total = perturb[m, 0, l, start : start + tile, :].astype(jnp.float32) * weighted[0]
                for v in range(1, variables):
                    total = total + perturb[m, v, l, start : start + tile, :].astype(jnp.float32) * weighted[v]
                base = (m * levels + l) * rows
                back[base + start : base + start + tile, :] = total
        slot, sub = divmod(l * STEPS, SUBLANES)
        slot += levels * 2 * STEPS + levels
        counts = ordered(odd, got_far[slot, sub : sub + STEPS, :], got_near[slot, sub : sub + STEPS, :])
        counts = [jnp.concatenate([c, c], axis=0) * (scale * scale) for c in counts]
        totals = [[0.0] * pairs, [0.0] * pairs]
        for v in range(variables):
            both = increment[grid.tile_of(increment, v * levels + l, rows // SUBLANES)]
            after = jnp.where(upper(), both, turned(both))
            before = jnp.where(upper(), turned(both), both)
            weighted = [c * (weights[v] * w) for c, w in zip(counts, (after, before))]
            for q in range(pairs):
                at = (v * levels + l) * pairs + q
                for side, p in enumerate(ordered(odd, rim_far[at], rim_near[at])):
                    totals[side][q] = totals[side][q] + p * weighted[side]
        for q in range(pairs):
            at = slice((l * pairs + q) * SUBLANES, (l * pairs + q + 1) * SUBLANES)
            back_after[at, :] = totals[0][q]
            back_before[at, :] = totals[1][q]
    field_columns(grid, lambda l, k: grid.ring_row(back, back_before, back_after, l, k), grid.ring, near, far, edges)


def adjoint_kernel(grid, control, main, edges, strip_ring, col_near, col_far, out_hbm, strip_keep, ends, out, sems):
    results = strip_steps(grid, adjoint_steps, edges, grid.ring, STEPS, col_near, col_far, strip_ring, strip_keep)
    for y, value in enumerate(results):
        ends[pl.ds(y, grid.members, stride=grid.rows), :] = value
    planes = (grid.members * grid.levels, grid.rows, LANES)
    copies = []
    for start in range(0, grid.rows, SUBLANES):
        for m in range(grid.members):
            end = ends[pl.ds(m * grid.rows + start, SUBLANES), :]
            for l in range(grid.levels):
                at = pl.ds((m * grid.levels + l) * grid.rows + start, SUBLANES)
                out[at, :] = control[at, :] + merged(grid, main[at, :], end, l)
        part = pl.ds(start, SUBLANES)
        copies.append(pltpu.make_async_copy(out.reshape(planes).at[:, part, :], out_hbm.at[:, part, :], sems.at[start // SUBLANES]))
        copies[-1].start()
    for copy in copies:
        copy.wait()


def shape_of(*shape):
    return jax.ShapeDtypeStruct(shape, jnp.float32)


def shards(control, perturb, obs_count, obs_weight, diffusivity):
    members, levels, rows, lanes = control.shape
    variables = perturb.shape[1]
    ways = lax.axis_size("mem")
    scale = 1.0 / math.sqrt(members * ways - 1)
    count = members * levels
    grid = Grid(members, levels, rows)
    assert members == SUBLANES and lanes == LANES and grid.block >= 8 * STEPS
    vmem = pl.BlockSpec(memory_space=pltpu.VMEM)
    hbm = pl.BlockSpec(memory_space=pltpu.HBM)
    f32 = jnp.float32

    def call(kernel, *args, work=0, **kwargs):
        cost = pl.CostEstimate(flops=work, bytes_accessed=work, transcendentals=0) if work else None
        return pl.pallas_call(
            lambda *refs: kernel(grid, *refs), compiler_params=PARAMS, cost_estimate=cost, **kwargs
        )(*args)

    def in_hbm(array):
        return pltpu.with_memory_space_constraint(array, pltpu.HBM)

    depth = 2 * STEPS
    ring_shape, strip_shape = (levels * grid.wide, lanes), (grid.padded, lanes)
    rim = shape_of(count * STEPS, lanes)

    def tiles(number):
        return shape_of(number, SUBLANES, lanes)

    edge = tiles(levels * depth + levels + -(-levels * STEPS // SUBLANES))
    outer = tiles(variables * levels * members // 2)
    level_rows = shape_of(levels * rows, lanes)
    edge_rows = pltpu.VMEM((members, variables, levels, SUBLANES, lanes), perturb.dtype)
    near, far, outer_near, outer_far, flat, flat_diff, seen, weights = call(
        rows_kernel,
        in_hbm(control.reshape(count * rows, lanes)),
        in_hbm(diffusivity.reshape(levels * rows, lanes)),
        in_hbm(obs_count.reshape(levels * rows, lanes)),
        in_hbm(obs_weight),
        in_hbm(perturb),
        out_shape=(edge, edge, outer, outer, shape_of(count * rows, lanes), level_rows, level_rows, tiles(variables)),
        in_specs=[hbm] * 5,
        scratch_shapes=[
            pltpu.VMEM(level_rows.shape, jnp.int32),
            pltpu.SMEM(obs_weight.shape, f32),
            edge_rows,
            edge_rows,
            pltpu.SemaphoreType.DMA((6,)),
        ],
    )
    got = swap(near, far, "gy")
    rims = swap(outer_near, outer_far, "gy")
    edge = tiles(grid.wide_packs + 1)
    near, far, edges, ring, ring_edges = call(
        columns_kernel,
        flat,
        flat_diff,
        *got,
        out_shape=(edge, edge, tiles(grid.wide), shape_of(*ring_shape), shape_of(*strip_shape)),
    )
    sides = swap(near, far, "gx")
    *main, held = call(
        spread_main_kernel,
        flat,
        ring,
        *got,
        in_hbm(perturb),
        work=6 << 20,
        out_shape=(shape_of(count * rows, lanes), rim, rim, jax.ShapeDtypeStruct(perturb.shape, perturb.dtype)),
        in_specs=[vmem] * 4 + [hbm],
        scratch_shapes=[pltpu.VMEM(ring_shape, f32), pltpu.SemaphoreType.DMA],
    )
    piece = -(-variables * levels * grid.ring // (ways * SUBLANES)) * SUBLANES
    partial, strip_ring = call(
        spread_kernel,
        *main,
        edges,
        ring_edges,
        *sides,
        held,
        *rims,
        out_shape=(shape_of(ways, piece, lanes), shape_of(*strip_shape)),
        scratch_shapes=[
            pltpu.VMEM(strip_shape, f32),
            pltpu.VMEM((members * rows, lanes), f32),
            pltpu.VMEM((members * STEPS, lanes), f32),
            pltpu.VMEM((members * STEPS, lanes), f32),
        ],
    )

    parts = lax.all_to_all(partial, "mem", 0, 0)
    mine = jnp.sum(parts, axis=0)
    increment = lax.all_to_all(jnp.broadcast_to(mine, parts.shape), "mem", 0, 0)

    edge = tiles(grid.packs)
    back, before, after, edges, near, far = call(
        lambda grid, *refs: back_kernel(grid, scale, *refs),
        increment,
        seen,
        weights,
        held,
        *rims,
        *got,
        out_shape=(shape_of(count * rows, lanes), rim, rim, tiles(grid.ring), edge, edge),
    )
    sides = swap(near, far, "gx")
    main = call(
        adjoint_main_kernel,
        back,
        before,
        after,
        ring,
        work=6 << 20,
        out_shape=shape_of(count * rows, lanes),
        scratch_shapes=[pltpu.VMEM(ring_shape, f32)],
    )
    out = call(
        adjoint_kernel,
        flat,
        main,
        edges,
        strip_ring,
        *sides,
        out_shape=shape_of(count, rows, lanes),
        out_specs=hbm,
        scratch_shapes=[
            pltpu.VMEM(strip_shape, f32),
            pltpu.VMEM((members * rows, lanes), f32),
            pltpu.VMEM((count * rows, lanes), f32),
            pltpu.SemaphoreType.DMA((rows // SUBLANES,)),
        ],
    )
    return out.reshape(control.shape)


def solution(mesh):
    placed = (
        P("mem", None, "gy", "gx"),
        P("mem", None, None, "gy", "gx"),
        P(None, "gy", "gx"),
        P(),
        P(None, "gy", "gx"),
    )

    return jax.shard_map(shards, mesh=mesh, in_specs=placed, out_specs=P("mem", None, "gy", "gx"), check_vma=False)
```

```python
import math

import jax
import jax.numpy as jnp
from jax import lax
from jax.experimental import pallas as pl
from jax.experimental.pallas import tpu as pltpu
from jax.sharding import PartitionSpec as P


STEPS = 4
LANES = 128
SUBLANES = 8
PARAMS = pltpu.CompilerParams(vmem_limit_bytes=16 << 20)


def swap(near, far, axis):
    size = lax.axis_size(axis)
    out = []
    for value, start in ((near, 0), (far, 1)):
        pairs = []
        for i in range(start, size - 1, 2):
            pairs += [(i, i + 1), (i + 1, i)]
        out.append(lax.ppermute(value, axis, pairs))
    return out


def is_odd(axis):
    return lax.rem(lax.axis_index(axis), 2) == 1


def ordered(odd, first, last):
    return jnp.where(odd, first, last), jnp.where(odd, last, first)


class Grid:
    def __init__(self, members, levels, rows):
        self.members, self.levels, self.rows = members, levels, rows
        self.wide = rows + 4 * STEPS
        self.ring = rows + 2 * STEPS
        self.block = LANES // levels // STEPS * STEPS
        self.per = self.block // STEPS
        self.wide_packs = -(-self.wide // self.per)
        self.packs = -(-self.ring // self.per)
        self.padded = self.per * SUBLANES

    def members_at(self, level, y):
        return pl.ds(level * self.rows + y, self.members, stride=self.levels * self.rows)

    def rim_at(self, level, r):
        return pl.ds(level * self.members * STEPS + r, self.members, stride=STEPS)

    def wide_row(self, field, got, odd, level, k):
        y = k - 2 * STEPS
        if 0 <= y < self.rows:
            return field[self.members_at(level, y), :]
        before = y < 0
        at = level * 2 * STEPS + (k if before else y - self.rows)
        near, far = got
        after_value, before_value = ordered(odd, far[at], near[at])
        return before_value if before else after_value

    def ring_row(self, field, before, after, level, k):
        y = k - STEPS
        if y < 0:
            return before[self.rim_at(level, k), :]
        if y >= self.rows:
            return after[self.rim_at(level, y - self.rows), :]
        return field[self.members_at(level, y), :]

    def set_ring_row(self, field, before, after, level, k, value):
        y = k - STEPS
        if y < 0:
            before[self.rim_at(level, k), :] = value
        elif y >= self.rows:
            after[self.rim_at(level, y - self.rows), :] = value
        else:
            field[self.members_at(level, y), :] = value

    def tile_of(self, ref, plane, j):
        t = plane * (self.ring // SUBLANES) + j
        return t // (ref.shape[1] // SUBLANES), pl.ds(t % (ref.shape[1] // SUBLANES) * SUBLANES, SUBLANES)

    def lanes(self, rows=SUBLANES):
        lane = lax.broadcasted_iota(jnp.int32, (rows, LANES), 1)
        return lax.rem(lane, self.block)


def within(place, start, size):
    return (place >= start) & (place < start + size)


def rolled(value, shift):
    shift %= LANES
    return pltpu.roll(value, shift, 1) if shift else value


def edges_of(grid, value_of, rows=SUBLANES):
    lane = lax.broadcasted_iota(jnp.int32, (rows, LANES), 1)
    out = jnp.zeros((rows, LANES), jnp.float32)
    for l in range(grid.levels):
        base = l * grid.block
        out = jnp.where(within(lane, base, 4 * STEPS), rolled(value_of(l), base + 2 * STEPS), out)
    return out


def packed(grid, edges, rows=SUBLANES):
    place = grid.lanes(rows)
    first = jnp.zeros((rows, LANES), jnp.float32)
    last = first
    for i, value in enumerate(edges):
        mask = within(place, i * STEPS, STEPS)
        first = jnp.where(mask, rolled(value, (i - 2) * STEPS), first)
        last = jnp.where(mask, rolled(value, (i - 1) * STEPS), last)
    return first, last


def strip_of(grid, edges, west, east, i, rows=SUBLANES):
    place = grid.lanes(rows)
    out = jnp.where(place < 2 * STEPS, edges, 0.0)
    out = jnp.where(within(place, 6 * STEPS, 2 * STEPS), rolled(edges, 4 * STEPS), out)
    out = jnp.where(within(place, 2 * STEPS, STEPS), rolled(east, (2 - i) * STEPS), out)
    return jnp.where(within(place, 5 * STEPS, STEPS), rolled(west, (5 - i) * STEPS), out)


def joined(grid, strip):
    return jnp.where(grid.lanes() < 2 * STEPS, strip, rolled(strip, -4 * STEPS))


def merged(grid, main, ends, level):
    lane = lax.broadcasted_iota(jnp.int32, main.shape, 1)
    outer = (lane < STEPS) | (lane >= LANES - STEPS)
    return jnp.where(outer, rolled(ends, LANES - 2 * STEPS - level * grid.block), main)


def lateral(value):
    return pltpu.roll(value, 1, 1) + pltpu.roll(value, LANES - 1, 1)


def spread_steps(field, coef, keep):
    for s in range(1, STEPS + 1):
        new = list(field)
        for k in range(s, len(field) - s):
            around = (field[k - 1] + field[k + 1]) + lateral(field[k])
            new[k] = keep(k) * field[k] + coef(k) * around
        field = new
    return field[STEPS:-STEPS]


def adjoint_steps(field, coef, keep):
    for s in range(1, STEPS + 1):
        flux = {k: coef(k) * field[k] for k in range(s - 1, len(field) - s + 1)}
        new = list(field)
        for k in range(s, len(field) - s):
            new[k] = keep(k) * field[k] + ((flux[k - 1] + flux[k + 1]) + lateral(flux[k]))
        field = new
    return field[STEPS:-STEPS]


def row_reader(ref, start):
    return lambda k: jnp.broadcast_to(ref[pl.ds(start + k, 1), :], (SUBLANES, LANES))


def turned(value):
    return pltpu.roll(value, STEPS, 0)


def upper():
    return lax.broadcasted_iota(jnp.int32, (SUBLANES, LANES), 0) < STEPS


def rows_kernel(
    grid,
    control_hbm,
    diffusivity_hbm,
    count_hbm,
    weight_hbm,
    perturb_hbm,
    near,
    far,
    outer_near,
    outer_far,
    own_edges,
    control,
    diffusivity,
    seen,
    weights,
    count,
    weight,
    heads,
    tails,
    sems,
):
    levels, rows = grid.levels, grid.rows
    depth = 2 * STEPS
    pairs = (
        (diffusivity_hbm, diffusivity),
        (count_hbm, count),
        (weight_hbm, weight),
        (control_hbm, control),
        (perturb_hbm.at[:, :, :, pl.ds(0, SUBLANES), :], heads),
        (perturb_hbm.at[:, :, :, pl.ds(rows - SUBLANES, SUBLANES), :], tails),
    )
    copies = [pltpu.make_async_copy(source, target, sems.at[i]) for i, (source, target) in enumerate(pairs)]
    for copy in copies:
        copy.start()
    odd = is_odd("gy")
    for copy in copies[:3]:
        copy.wait()
    for v in range(weights.shape[0]):
        weights[v] = jnp.full((SUBLANES, LANES), weight[v])
    seen[...] = count[...].astype(jnp.float32)
    at = levels * depth
    for l in range(levels):
        first = diffusivity[l * rows : l * rows + depth, :]
        last = diffusivity[(l + 1) * rows - depth : (l + 1) * rows, :]
        near[at + l], far[at + l] = ordered(odd, first, last)
        first = seen[l * rows : l * rows + STEPS, :]
        last = seen[(l + 1) * rows - STEPS : (l + 1) * rows, :]
        slot, sub = divmod(l * STEPS, SUBLANES)
        a, b = ordered(odd, first, last)
        near[at + levels + slot, sub : sub + STEPS, :] = a
        far[at + levels + slot, sub : sub + STEPS, :] = b
    copies[3].wait()
    for l in range(levels):
        for r in range(depth):
            first = control[grid.members_at(l, r), :]
            last = control[grid.members_at(l, rows - depth + r), :]
            near[l * depth + r], far[l * depth + r] = ordered(odd, first, last)
    for y in range(rows):
        own_edges[y] = edges_of(grid, lambda l: control[grid.members_at(l, y), :])
    copies[4].wait()
    copies[5].wait()
    members, variables = heads.shape[:2]
    for q in range(members // 2):
        for v in range(variables):
            for l in range(levels):
                head = [heads[2 * q + j, v, l].astype(jnp.float32) for j in range(2)]
                tail = [tails[2 * q + j, v, l].astype(jnp.float32) for j in range(2)]
                first = jnp.where(upper(), head[0], turned(head[1]))
                last = jnp.where(upper(), turned(tail[0]), tail[1])
                at = (v * levels + l) * (members // 2) + q
                outer_near[at], outer_far[at] = ordered(odd, first, last)


def field_columns(grid, edges_at, length, near, far, edges):
    for start in range(0, length, grid.per):
        here = []
        for k in range(start, min(length, start + grid.per)):
            here.append(edges_at(k))
            edges[k] = here[-1]
        q = start // grid.per
        near[q], far[q] = ordered(is_odd("gx"), *packed(grid, here))


def columns_kernel(grid, own_edges, control, diffusivity, got_near, got_far, near, far, edges, ring, ring_edges):
    got = (got_near, got_far)
    odd = is_odd("gy")
    depth = 2 * STEPS

    def edges_at(k):
        if depth <= k < depth + grid.rows:
            return own_edges[k - depth]
        return edges_of(grid, lambda l: grid.wide_row(control, got, odd, l, k))

    field_columns(grid, edges_at, grid.wide, near, far, edges)
    for l in range(grid.levels):
        after, before = ordered(odd, got_far[grid.levels * depth + l], got_near[grid.levels * depth + l])
        base = l * grid.wide
        ring[base : base + depth, :] = before
        ring[base + depth : base + depth + grid.rows, :] = diffusivity[l * grid.rows : (l + 1) * grid.rows, :]
        ring[base + depth + grid.rows : base + grid.wide, :] = after
    ring_edges[...] = jnp.zeros(ring_edges.shape, jnp.float32)
    ring_edges[: grid.wide, :] = edges_of(grid, lambda l: ring[l * grid.wide : (l + 1) * grid.wide, :], grid.wide)
    packs = grid.wide_packs
    spaced = [ring_edges[pl.ds(i, packs, stride=grid.per), :] for i in range(grid.per)]
    a, b = ordered(is_odd("gx"), *packed(grid, spaced, packs))
    near[packs, :packs, :] = a
    far[packs, :packs, :] = b


def spread_main_kernel(grid, control, ring, got_near, got_far, perturb_hbm, main, main_before, main_after, perturb, keep, sem):
    copy = pltpu.make_async_copy(perturb_hbm, perturb, sem)
    copy.start()
    odd = is_odd("gy")
    keep[...] = 1.0 - 4.0 * ring[...]
    for l in range(grid.levels):
        rows = [grid.wide_row(control, (got_near, got_far), odd, l, k) for k in range(grid.wide)]
        at = l * grid.wide
        for k, row in enumerate(spread_steps(rows, row_reader(ring, at), row_reader(keep, at))):
            grid.set_ring_row(main, main_before, main_after, l, k, row)
    copy.wait()


def adjoint_main_kernel(grid, back, before, after, ring, main, keep):
    keep[...] = 1.0 - 4.0 * ring[...]
    for l in range(grid.levels):
        rows = [grid.ring_row(back, before, after, l, k) for k in range(grid.ring)]
        at = l * grid.wide + STEPS
        for y, row in enumerate(adjoint_steps(rows, row_reader(ring, at), row_reader(keep, at))):
            main[grid.members_at(l, y), :] = row


def sides(col_near, col_far, q):
    east, west = ordered(is_odd("gx"), col_far[q], col_near[q])
    return west, east


def strip_steps(grid, steps, edges, length, skip, col_near, col_far, strip_ring, strip_keep):
    strip_keep[...] = 1.0 - 4.0 * strip_ring[...]
    field = []
    for k in range(length):
        q, i = divmod(k, grid.per)
        field.append(strip_of(grid, edges[k], *sides(col_near, col_far, q), i))
    return [joined(grid, strip) for strip in steps(field, row_reader(strip_ring, skip), row_reader(strip_keep, skip))]


def spread_kernel(
    grid,
    main,
    main_before,
    main_after,
    edges,
    ring_edges,
    col_near,
    col_far,
    perturb,
    rim_near,
    rim_far,
    partial,
    strip_ring,
    strip_keep,
    ends,
    ends_before,
    ends_after,
):
    packs = grid.wide_packs
    west, east = (side[:packs] for side in sides(col_near, col_far, packs))
    strip_ring[...] = jnp.zeros(strip_ring.shape, jnp.float32)
    for i in range(grid.per):
        at = pl.ds(i, packs, stride=grid.per)
        strip_ring[at, :] = strip_of(grid, ring_edges[at, :], west, east, i, packs)
    members, variables, levels, rows, _ = perturb.shape
    one = Grid(members, 1, rows)
    for k, value in enumerate(strip_steps(grid, spread_steps, edges, grid.wide, 0, col_near, col_far, strip_ring, strip_keep)):
        one.set_ring_row(ends, ends_before, ends_after, 0, k, value)
    tile = 2 * SUBLANES
    odd = is_odd("gy")
    pairs = members // 2
    for l in range(levels):
        for start in range(0, rows, tile):
            here = []
            for m in range(members):
                at = pl.ds((m * levels + l) * rows + start, tile)
                here.append(merged(grid, main[at, :], ends[pl.ds(m * rows + start, tile), :], l))
            for v in range(variables):
                total = perturb[0, v, l, start : start + tile, :].astype(jnp.float32) * here[0]
                for m in range(1, members):
                    total = total + perturb[m, v, l, start : start + tile, :].astype(jnp.float32) * here[m]
                for j in range(2):
                    partial[grid.tile_of(partial, v * levels + l, start // SUBLANES + j)] = total[j * SUBLANES : (j + 1) * SUBLANES]
        rims = []
        for q in range(pairs):
            at, end_at = pl.ds((l * pairs + q) * SUBLANES, SUBLANES), pl.ds(q * SUBLANES, SUBLANES)
            both = ((main_after, ends_after), (main_before, ends_before))
            rims.append([merged(grid, m[at, :], e[end_at, :], l) for m, e in both])
        for v in range(variables):
            totals = [0.0, 0.0]
            for q in range(pairs):
                at = (v * levels + l) * pairs + q
                outer = ordered(odd, rim_far[at], rim_near[at])
                totals = [t + p * r for t, p, r in zip(totals, outer, rims[q])]
            after, before = (t + turned(t) for t in totals)
            partial[grid.tile_of(partial, v * levels + l, rows // SUBLANES)] = jnp.where(upper(), after, before)
    used = variables * levels * (grid.ring // SUBLANES)
    for t in range(used, partial.shape[0] * partial.shape[1] // SUBLANES):
        partial[grid.tile_of(partial, 0, t)] = jnp.zeros((SUBLANES, LANES), jnp.float32)


def back_kernel(
    grid,
    scale,
    increment,
    seen,
    weights,
    perturb,
    rim_near,
    rim_far,
    got_near,
    got_far,
    back,
    back_before,
    back_after,
    edges,
    near,
    far,
):
    members, variables, levels, rows, _ = perturb.shape
    tile = 2 * SUBLANES
    odd = is_odd("gy")
    pairs = members // 2
    for l in range(levels):
        for start in range(0, rows, tile):
            factor = seen[l * rows + start : l * rows + start + tile, :] * (scale * scale)
            weighted = []
            for v in range(variables):
                at = [grid.tile_of(increment, v * levels + l, start // SUBLANES + j) for j in range(2)]
                pair = [weights[v] * increment[a] for a in at]
                weighted.append(factor * jnp.concatenate(pair, axis=0))
            for m in range(members):
                total = perturb[m, 0, l, start : start + tile, :].astype(jnp.float32) * weighted[0]
                for v in range(1, variables):
                    total = total + perturb[m, v, l, start : start + tile, :].astype(jnp.float32) * weighted[v]
                base = (m * levels + l) * rows
                back[base + start : base + start + tile, :] = total
        slot, sub = divmod(l * STEPS, SUBLANES)
        slot += levels * 2 * STEPS + levels
        counts = ordered(odd, got_far[slot, sub : sub + STEPS, :], got_near[slot, sub : sub + STEPS, :])
        counts = [jnp.concatenate([c, c], axis=0) * (scale * scale) for c in counts]
        totals = [[0.0] * pairs, [0.0] * pairs]
        for v in range(variables):
            both = increment[grid.tile_of(increment, v * levels + l, rows // SUBLANES)]
            after = jnp.where(upper(), both, turned(both))
            before = jnp.where(upper(), turned(both), both)
            weighted = [c * (weights[v] * w) for c, w in zip(counts, (after, before))]
            for q in range(pairs):
                at = (v * levels + l) * pairs + q
                for side, p in enumerate(ordered(odd, rim_far[at], rim_near[at])):
                    totals[side][q] = totals[side][q] + p * weighted[side]
        for q in range(pairs):
            at = slice((l * pairs + q) * SUBLANES, (l * pairs + q + 1) * SUBLANES)
            back_after[at, :] = totals[0][q]
            back_before[at, :] = totals[1][q]

    def edges_at(k):
        return edges_of(grid, lambda l: grid.ring_row(back, back_before, back_after, l, k))

    field_columns(grid, edges_at, grid.ring, near, far, edges)


def adjoint_kernel(grid, control, main, edges, strip_ring, col_near, col_far, out_hbm, strip_keep, ends, out, sems):
    results = strip_steps(grid, adjoint_steps, edges, grid.ring, STEPS, col_near, col_far, strip_ring, strip_keep)
    for y, value in enumerate(results):
        ends[pl.ds(y, grid.members, stride=grid.rows), :] = value
    planes = (grid.members * grid.levels, grid.rows, LANES)
    copies = []
    for start in range(0, grid.rows, SUBLANES):
        for m in range(grid.members):
            end = ends[pl.ds(m * grid.rows + start, SUBLANES), :]
            for l in range(grid.levels):
                at = pl.ds((m * grid.levels + l) * grid.rows + start, SUBLANES)
                out[at, :] = control[at, :] + merged(grid, main[at, :], end, l)
        part = pl.ds(start, SUBLANES)
        copies.append(pltpu.make_async_copy(out.reshape(planes).at[:, part, :], out_hbm.at[:, part, :], sems.at[start // SUBLANES]))
        copies[-1].start()
    for copy in copies:
        copy.wait()


def shape_of(*shape):
    return jax.ShapeDtypeStruct(shape, jnp.float32)


def shards(control, perturb, obs_count, obs_weight, diffusivity):
    members, levels, rows, lanes = control.shape
    variables = perturb.shape[1]
    ways = lax.axis_size("mem")
    scale = 1.0 / math.sqrt(members * ways - 1)
    count = members * levels
    grid = Grid(members, levels, rows)
    assert members == SUBLANES and lanes == LANES and grid.block >= 8 * STEPS
    vmem = pl.BlockSpec(memory_space=pltpu.VMEM)
    hbm = pl.BlockSpec(memory_space=pltpu.HBM)
    f32 = jnp.float32

    def call(kernel, *args, work=0, **kwargs):
        cost = pl.CostEstimate(flops=work, bytes_accessed=work, transcendentals=0) if work else None
        return pl.pallas_call(
            lambda *refs: kernel(grid, *refs), compiler_params=PARAMS, cost_estimate=cost, **kwargs
        )(*args)

    def in_hbm(array):
        return pltpu.with_memory_space_constraint(array, pltpu.HBM)

    depth = 2 * STEPS
    ring_shape, strip_shape = (levels * grid.wide, lanes), (grid.padded, lanes)
    rim = shape_of(count * STEPS, lanes)

    def tiles(number):
        return shape_of(number, SUBLANES, lanes)

    edge = tiles(levels * depth + levels + -(-levels * STEPS // SUBLANES))
    outer = tiles(variables * levels * members // 2)
    level_rows = shape_of(levels * rows, lanes)
    edge_rows = pltpu.VMEM((members, variables, levels, SUBLANES, lanes), perturb.dtype)
    near, far, outer_near, outer_far, own_edges, flat, flat_diff, seen, weights = call(
        rows_kernel,
        in_hbm(control.reshape(count * rows, lanes)),
        in_hbm(diffusivity.reshape(levels * rows, lanes)),
        in_hbm(obs_count.reshape(levels * rows, lanes)),
        in_hbm(obs_weight),
        in_hbm(perturb),
        out_shape=(edge, edge, outer, outer, tiles(rows), shape_of(count * rows, lanes), level_rows, level_rows, tiles(variables)),
        in_specs=[hbm] * 5,
        scratch_shapes=[
            pltpu.VMEM(level_rows.shape, jnp.int32),
            pltpu.SMEM(obs_weight.shape, f32),
            edge_rows,
            edge_rows,
            pltpu.SemaphoreType.DMA((6,)),
        ],
    )
    got = swap(near, far, "gy")
    rims = swap(outer_near, outer_far, "gy")
    edge = tiles(grid.wide_packs + 1)
    near, far, edges, ring, ring_edges = call(
        columns_kernel,
        own_edges,
        flat,
        flat_diff,
        *got,
        out_shape=(edge, edge, tiles(grid.wide), shape_of(*ring_shape), shape_of(*strip_shape)),
    )
    sides = swap(near, far, "gx")
    *main, held = call(
        spread_main_kernel,
        flat,
        ring,
        *got,
        in_hbm(perturb),
        work=6 << 20,
        out_shape=(shape_of(count * rows, lanes), rim, rim, jax.ShapeDtypeStruct(perturb.shape, perturb.dtype)),
        in_specs=[vmem] * 4 + [hbm],
        scratch_shapes=[pltpu.VMEM(ring_shape, f32), pltpu.SemaphoreType.DMA],
    )
    piece = -(-variables * levels * grid.ring // (ways * SUBLANES)) * SUBLANES
    partial, strip_ring = call(
        spread_kernel,
        *main,
        edges,
        ring_edges,
        *sides,
        held,
        *rims,
        out_shape=(shape_of(ways, piece, lanes), shape_of(*strip_shape)),
        scratch_shapes=[
            pltpu.VMEM(strip_shape, f32),
            pltpu.VMEM((members * rows, lanes), f32),
            pltpu.VMEM((members * STEPS, lanes), f32),
            pltpu.VMEM((members * STEPS, lanes), f32),
        ],
    )

    parts = lax.all_to_all(partial, "mem", 0, 0)
    mine = jnp.sum(parts, axis=0)
    increment = lax.all_to_all(jnp.broadcast_to(mine, parts.shape), "mem", 0, 0)

    edge = tiles(grid.packs)
    back, before, after, edges, near, far = call(
        lambda grid, *refs: back_kernel(grid, scale, *refs),
        increment,
        seen,
        weights,
        held,
        *rims,
        *got,
        out_shape=(shape_of(count * rows, lanes), rim, rim, tiles(grid.ring), edge, edge),
    )
    sides = swap(near, far, "gx")
    main = call(
        adjoint_main_kernel,
        back,
        before,
        after,
        ring,
        work=6 << 20,
        out_shape=shape_of(count * rows, lanes),
        scratch_shapes=[pltpu.VMEM(ring_shape, f32)],
    )
    out = call(
        adjoint_kernel,
        flat,
        main,
        edges,
        strip_ring,
        *sides,
        out_shape=shape_of(count, rows, lanes),
        out_specs=hbm,
        scratch_shapes=[
            pltpu.VMEM(strip_shape, f32),
            pltpu.VMEM((members * rows, lanes), f32),
            pltpu.VMEM((count * rows, lanes), f32),
            pltpu.SemaphoreType.DMA((rows // SUBLANES,)),
        ],
    )
    return out.reshape(control.shape)


def solution(mesh):
    placed = (
        P("mem", None, "gy", "gx"),
        P("mem", None, None, "gy", "gx"),
        P(None, "gy", "gx"),
        P(),
        P(None, "gy", "gx"),
    )

    return jax.shard_map(shards, mesh=mesh, in_specs=placed, out_specs=P("mem", None, "gy", "gx"), check_vma=False)
```
